512 devices in a mesh: dp: 16 (over z), tensor: 32 (over x, y, core).
Axes of the slice: x: 4, y: 4, z: 16, core: 2. Of those that a mesh axis runs over, the one named last changes fastest.
Arguments:
- pages: bfloat16 [2, 64, 64, 2048], P(None, 'dp', None, 'tensor'), may hold values from -8 to 8
- page_table: int32 [16, 2], replicated, may hold values from 0 to 63, as said below
- page_count: int32 [16], replicated, may hold values from 1 to 2
- last_len: int32 [16], replicated, may hold values from 1 to 64
- targets: int32 [16, 128], P('dp'), may hold values from 0 to 65535
- mix_key: float32 [2, 2048], P(None, 'tensor'), may hold values from 0.05 to 0.95
- w_key: bfloat16 [2, 2048, 8192], P(None, None, 'tensor'), may hold values from -0.125 to 0.125
- w_value: bfloat16 [2, 8192, 2048], P(None, 'tensor'), may hold values from -0.0625 to 0.0625
- ln_gain: float32 [2, 2048], replicated, may hold values from 0.5 to 1.5
- ln_bias: float32 [2, 2048], replicated, may hold values from -2 to 2
- head: bfloat16 [2, 2048, 65536], P(None, 'dp', 'tensor'), may hold values from -8 to 8
Outputs:
- token_logprob: float32 [16, 128], P('dp', 'tensor')
- ratio_sum: float32 [16], P('dp')
The draws below stay inside these ranges and needn't reach their ends.
Inputs may be any that keep to these rules, and one draw needn't show every extreme that they name: Entries are distinct; the page lives on dp device page_table[r, p] // 4.
All inputs are finite; a program needn't handle non-finite values.
Results may differ from the reference program's by a relative error of at most 0.0029.
The reference program's roundings to bfloat16 on the way (of `states`, `shifted`, `key_act` and `normed`) count: a program that leaves them out, or rounds other values in their place, can miss the bound.
Values may be sent and summed in bfloat16 or wider, within the bound.
A program may use at most 128 MiB of HBM per device.

```python
import math
import jax
import jax.numpy as jnp
from jax import lax

D = 2048
FF = 8192
VOCAB = 65536
PAGE = 64
MAXP = 2
ROLLS = 16
NPAGES = 64
SLOTS = 128


def signs_of(key):
    flips = jax.random.bernoulli(jax.random.fold_in(key, 101), 0.5, (D,))
    return jnp.where(flips, 1.0, -1.0).astype(jnp.float32)


def draw_pages(key, part):
    array_shape = (2, NPAGES, PAGE, D)
    feature = 0.6 * jnp.exp(jnp.log(3.0) * jnp.arange(D, dtype=jnp.float32) / D)
    values = jnp.clip(jax.random.normal(jax.random.fold_in(key, 1), array_shape, jnp.float32), -4.0, 4.0) * feature
    amplitude = jax.random.uniform(jax.random.fold_in(key, 2), (2, NPAGES, 1, 1), jnp.float32, 0.8, 1.2)
    leading = (jnp.arange(PAGE) < 2)[None, None, :, None]
    values = jnp.where(leading, signs_of(key)[None, None, None, :] * amplitude, values)
    return values.astype(jnp.bfloat16)


def draw_head(key, part):
    array_shape = (2, D, VOCAB)
    spread = 3.0 / math.sqrt(D)
    base_draw = jnp.clip(jax.random.normal(jax.random.fold_in(key, 4), array_shape, jnp.float32), -4.0, 4.0) * spread
    first_col = jax.random.randint(jax.random.fold_in(key, 5), (), 0, VOCAB - 1)
    column = jnp.arange(VOCAB)[None, None, :]
    aligned = signs_of(key)[None, :, None] * (400.0 / D)
    base_draw = jnp.where(column == first_col, aligned, jnp.where(column == first_col + 1, aligned * 1.006, base_draw))
    return base_draw.astype(jnp.bfloat16)


def draw_page_table(key, part):
    middle = 1 + jax.random.permutation(jax.random.fold_in(key, 7), NPAGES - 2)
    chosen_rows = jnp.concatenate([jnp.array([0, NPAGES - 1], jnp.int32), middle[:ROLLS * MAXP - 2].astype(jnp.int32)])
    shuffled = jax.random.permutation(jax.random.fold_in(key, 17), chosen_rows)
    return shuffled.reshape(ROLLS, MAXP).astype(jnp.int32)


def draw_page_count(key, part):
    first_draw = jax.random.randint(jax.random.fold_in(key, 8), (ROLLS,), 0, MAXP)
    second_draw = jax.random.randint(jax.random.fold_in(key, 9), (ROLLS,), 0, MAXP)
    counts = 1 + first_draw * second_draw // (MAXP - 1)
    chosen = jax.random.randint(jax.random.fold_in(key, 10), (), 0, ROLLS)
    return jnp.where(jnp.arange(ROLLS) == chosen, MAXP, counts).astype(jnp.int32)


def draw_last_len(key, part):
    lengths = jax.random.randint(jax.random.fold_in(key, 12), (ROLLS,), 1, PAGE + 1)
    chosen = jax.random.randint(jax.random.fold_in(key, 13), (), 0, ROLLS)
    return jnp.where(jnp.arange(ROLLS) == chosen, PAGE, lengths).astype(jnp.int32)


def plant(values, own_key, low, high):
    dims = values.shape
    place = [jax.random.randint(jax.random.fold_in(own_key, axis), (), 0, dims[axis]) for axis in range(len(dims))]
    values = values.at[tuple(place)].set(low)
    longest = dims.index(max(dims))
    place[longest] = (place[longest] + 1) % dims[longest]
    return values.at[tuple(place)].set(high)


def level_of(own_key, dims, split, smallest, top_value):
    gain = 1.0
    for position, parts in split:
        heights = jax.random.uniform(jax.random.fold_in(jax.random.fold_in(own_key, 6), position), (parts,), jnp.float32, smallest / len(split), top_value / len(split))
        gain = gain * jnp.repeat(jnp.exp(heights), dims[position] // parts).reshape((-1,) + (1,) * (len(dims) - 1 - position))
    return gain


def bell_draw(key, dims, width, limit, cuts=(), kind=jnp.bfloat16):
    values = jax.random.normal(key, dims, jnp.float32) * width
    if len(cuts) > 0:
        values = level_of(key, dims, cuts, -0.22, 0.18) * values
    return jnp.clip(values, min=-limit, max=limit).astype(kind)


def setup_inputs(seed: int = 0) -> dict:
    keys = jax.random.split(jax.random.key(seed), 12)
    return {
        "pages": draw_pages(jax.random.fold_in(keys[11], 71), 0),
        "page_table": draw_page_table(jax.random.fold_in(keys[11], 71), 0),
        "page_count": draw_page_count(jax.random.fold_in(keys[11], 71), 0),
        "last_len": draw_last_len(jax.random.fold_in(keys[11], 71), 0),
        "targets": plant(jax.random.randint(keys[4], (ROLLS, SLOTS), 0, VOCAB), jax.random.fold_in(keys[4], 1), 0, VOCAB - 1).astype(jnp.int32),
        "mix_key": jnp.clip(0.05 + 0.9 * jax.random.uniform(keys[5], (2, D), jnp.float32) ** level_of(keys[5], (2, D), ((1, 32),), -0.2, 0.2), 0.05, 0.95),
        "w_key": bell_draw(keys[6], (2, D, FF), D ** -0.5, 0.125, ((2, 32),)),
        "w_value": bell_draw(keys[7], (2, FF, D), FF ** -0.5, 0.0625, ((1, 32),)),
        "ln_gain": jnp.clip(1.0 + 0.1 * jax.random.normal(keys[8], (2, D), jnp.float32), 0.5, 1.5),
        "ln_bias": bell_draw(keys[9], (2, D), 0.3, 2.0, (), jnp.float32),
        "head": draw_head(jax.random.fold_in(keys[11], 71), 0),
    }


epsilon = 1e-05

def reference(pages, page_table, page_count, last_len, targets, mix_key, w_key, w_value, ln_gain, ln_bias, head):
    picked = pages[:, page_table]
    live = jnp.arange(MAXP)[None, :] < page_count[:, None]
    picked = jnp.where(live[None, :, :, None, None], picked, jnp.zeros_like(picked))
    states = jnp.transpose(picked.reshape(2, ROLLS, MAXP * PAGE, D), (1, 0, 2, 3))
    lengths = (page_count - 1) * PAGE + last_len
    key_full = w_key.astype(jnp.float32)
    value_full = w_value.astype(jnp.float32)
    head_full = head.astype(jnp.float32)

    def one_rollout(inputs):
        state, target_row, length = inputs
        state_f = state.astype(jnp.float32)
        previous = jnp.concatenate([jnp.zeros((2, 1, D), jnp.float32), state_f[:, :-1]], axis=1)
        shifted = (state_f + (previous - state_f) * mix_key[:, None, :]).astype(jnp.bfloat16)
        hidden = jnp.einsum('msd,mdf->msf', shifted.astype(jnp.float32), key_full)
        key_act = (jnp.maximum(hidden, 0.0) ** 2).astype(jnp.bfloat16)
        residual = state_f + jnp.einsum('msf,mfd->msd', key_act.astype(jnp.float32), value_full)
        average = lax.optimization_barrier(jnp.sum(residual, axis=-1)) / D
        variance = lax.optimization_barrier(jnp.sum(residual * residual, axis=-1)) / D - average * average
        normed = ((residual - average[..., None]) * lax.rsqrt(variance + epsilon)[..., None] * ln_gain[:, None, :] + ln_bias[:, None, :]).astype(jnp.bfloat16)
        logits = jnp.einsum('msd,mdv->msv', normed.astype(jnp.float32), head_full)
        peak = lax.optimization_barrier(jnp.max(logits, axis=-1))
        totals = lax.optimization_barrier(jnp.sum(jnp.exp(logits - peak[..., None]), axis=-1))
        target_logit = jnp.take_along_axis(logits, jnp.broadcast_to(target_row[None, :, None], (2, MAXP * PAGE, 1)), axis=2)[..., 0]
        logp = target_logit - peak - jnp.log(totals)
        valid = jnp.arange(MAXP * PAGE) < length
        token_row = jnp.where(valid, logp[0], 0.0)
        ratio = jnp.sum(jnp.where(valid, logp[0] - logp[1], 0.0))
        return (token_row, ratio)
    token_logprob, ratio_sum = lax.map(one_rollout, (states, targets, lengths))
    return (token_logprob, ratio_sum)
```

```python
import functools

import jax
import jax.numpy as jnp
from jax import lax
from jax.experimental import pallas as pl
from jax.experimental.pallas import tpu as pltpu
from jax.sharding import PartitionSpec as P

epsilon = 1e-05
F32 = jnp.float32
BF16 = jnp.bfloat16
LANES = 128


def iota(shape, axis):
    return lax.broadcasted_iota(jnp.int32, shape, axis)


def rows_of(*rows):
    place = iota((8, LANES), 0)
    tile = jnp.zeros((8, LANES), F32)
    for index, row in enumerate(rows):
        tile = jnp.where(place == index, jnp.broadcast_to(row, (8, LANES)), tile)
    return tile


def column_of(row):
    return jnp.broadcast_to(row, (LANES, LANES)).T


def kernel(
    nz,
    side,
    table_ref,
    count_ref,
    last_ref,
    pages_ref,
    mix_ref,
    target_ref,
    gain_ref,
    bias_ref,
    wk_hbm,
    wv_hbm,
    head_hbm,
    out_ref,
    pages_in,
    mix_in,
    targets_all,
    head_src,
    head_own,
    head_all,
    wk_all,
    wv_all,
    window,
    chosen,
    picked,
    shifted_all,
    act,
    partial,
    summed,
    stats,
    sets,
    tokens,
    logits,
    local_stats,
    column_stats,
    plane_stats,
    logp_pair,
    pair_send,
    pair_recv,
    load_sem,
    tgt_send,
    tgt_recv,
    win_send,
    win_recv,
    pick_send,
    pick_recv,
    shift_send,
    shift_recv,
    sum_send,
    sum_recv,
    stat_send,
    stat_recv,
    hz_send,
    hz_recv,
    hx_send,
    hx_recv,
    set_send,
    set_recv,
    near_send,
    near_recv,
    tok_send,
    tok_recv,
    c0_send,
    c0_recv,
    c1_send,
    c1_recv,
):
    chips = side * side
    per_set = nz // side
    z = lax.axis_index("dp")
    tensor = lax.axis_index("tensor")
    core = lax.rem(tensor, 2)
    chip = tensor // 2
    x = chip // side
    y = lax.rem(chip, side)
    my_set = lax.rem(x + y, side)
    z_set = lax.rem(z, side)
    sign = 1 - 2 * core
    width = chips * LANES
    units = wk_hbm.shape[2]
    vocab_half = head_hbm.shape[2]
    rows = head_hbm.shape[1]
    slots = nz // 2
    near = {4: (1, -1, 2), 2: (1,)}[side]

    def remote(src, dst, send, recv, to_z, to_chip, to_core):
        return pltpu.make_async_remote_copy(
            src_ref=src,
            dst_ref=dst,
            send_sem=send,
            recv_sem=recv,
            device_id={"dp": to_z, "tensor": to_chip * 2 + to_core},
            device_id_type=pl.DeviceIdType.MESH,
        )

    def wrap(value, size):
        return lax.rem(value + 4 * size, size)

    def lane(index):
        return pl.ds(pl.multiple_of(index * LANES, LANES), LANES)

    unit_cols = pl.ds(pl.multiple_of(core * units, units), units)
    loads = (
        pltpu.make_async_copy(wk_hbm.at[core], wk_all.at[:, unit_cols], load_sem.at[0]),
        pltpu.make_async_copy(wv_hbm.at[core], wv_all.at[unit_cols, :], load_sem.at[1]),
        pltpu.make_async_copy(head_hbm.at[core], head_src.at[core], load_sem.at[2]),
    )
    for load in loads:
        load.start()

    barrier = pltpu.get_barrier_semaphore()

    def hello(to_z, to_chip, to_core):
        pl.semaphore_signal(
            barrier,
            inc=1,
            device_id={"dp": to_z, "tensor": to_chip * 2 + to_core},
            device_id_type=pl.DeviceIdType.MESH,
        )

    hello(z, chip, 1 - core)

    def hello_z(step, carry):
        hello(wrap(z + step, nz), chip, core)
        return carry

    def hello_plane(step, carry):
        hello(z, wrap(chip + step, chips), core)
        return carry

    lax.fori_loop(1, nz, hello_z, 0)
    lax.fori_loop(1, chips, hello_plane, 0)
    pl.semaphore_wait(barrier, nz - 1 + chips - 1 + 1)

    other = 1 - core
    pair = (
        remote(pages_ref.at[other], pages_in, pair_send.at[0], pair_recv.at[0], z, chip, other),
        remote(mix_ref.at[other], mix_in, pair_send.at[1], pair_recv.at[1], z, chip, other),
        remote(
            head_hbm.at[other], head_src.at[core], pair_send.at[2], pair_recv.at[2], z, chip, other
        ),
        remote(
            wk_hbm.at[other],
            wk_all.at[:, unit_cols],
            pair_send.at[3],
            pair_recv.at[3],
            z,
            chip,
            other,
        ),
        remote(
            wv_hbm.at[other],
            wv_all.at[unit_cols, :],
            pair_send.at[4],
            pair_recv.at[4],
            z,
            chip,
            other,
        ),
    )
    for copy in pair:
        copy.start()

    pair[0].wait_recv()
    window[pl.ds(4, 4)] = pages_ref[core] + pages_in[...]
    window_offsets = {4: (-1, 0, 1, 2), 2: (-1, 0)}[side]
    mine = window.at[pl.ds(4, 4)]
    moves = []
    for slot, offset in enumerate(window_offsets):
        if offset == 0:
            continue
        copy = remote(
            mine,
            window.at[pl.ds(slot * 4, 4)],
            win_send.at[slot],
            win_recv.at[slot],
            wrap(z - sign * offset, nz),
            chip,
            core,
        )
        copy.start()
        moves.append(copy)
    targets_all[z] = target_ref[...]

    def send_target(step, carry):
        remote(
            target_ref,
            targets_all.at[z],
            tgt_send.at[step],
            tgt_recv.at[step],
            wrap(z + step, nz),
            chip,
            core,
        ).start()
        return carry

    lax.fori_loop(1, nz, send_target, 0)
    for copy in moves:
        copy.wait_recv()

    picks = []
    for step in range(per_set):
        to_z = wrap(z + side * step, nz)
        for page in range(2):
            entry = table_ref[to_z, page]
            slot = lax.rem((entry // 4 - z) * sign + 1 + 4 * nz, nz)
            wanted = jnp.logical_and(slot < side, page < count_ref[to_z])
            flag = jnp.where(wanted, 1.0, 0.0).astype(F32)
            index = jnp.minimum(slot, side - 1) * 4 + lax.rem(entry, 4)
            block = (window[index].astype(F32) * flag).astype(BF16)
            if step == 0:
                picked[0, page] = block
            else:
                chosen[step, page] = block
        if step > 0:
            copy = remote(
                chosen.at[step],
                picked.at[step],
                pick_send.at[step],
                pick_recv.at[step],
                to_z,
                chip,
                core,
            )
            copy.start()
            picks.append(copy)

    loads[2].wait()
    pair[2].wait_recv()

    def head_piece(to_z):
        start = pl.multiple_of(lax.rem(to_z, slots) * 2 * LANES, 2 * LANES)
        return head_src.at[to_z // slots, :, pl.ds(start, 2 * LANES)]

    def head_rows(index):
        return pl.ds(pl.multiple_of(index * rows, rows), rows)

    def head_copy(step):
        to_z = wrap(z + step, nz)
        return remote(
            head_piece(to_z),
            head_own.at[head_rows(z), :],
            hz_send.at[step],
            hz_recv.at[step],
            to_z,
            chip,
            core,
        )

    def head_start(step, carry):
        head_copy(step).start()
        return carry

    lax.fori_loop(1, nz, head_start, 0)
    keep = pltpu.make_async_copy(head_piece(z), head_own.at[head_rows(z), :], load_sem.at[3])
    keep.start()

    pair[1].wait_recv()
    for copy in picks:
        copy.wait_recv()
    state = picked[0].astype(F32)
    for step in range(1, per_set):
        state = state + picked[step].astype(F32)
    state = state.reshape(LANES, LANES)
    rolled = pltpu.roll(state, 1, 0)
    previous = jnp.where(iota((LANES, LANES), 0) == 0, 0.0, rolled)
    mix = mix_ref[core, 0:1, :] + mix_in[0:1, :]
    shifted_all[:, lane(chip)] = (state + (previous - state) * mix).astype(BF16)

    def shift_copy(step, source, to_chip):
        return remote(
            shifted_all.at[:, lane(source)],
            shifted_all.at[:, lane(source)],
            shift_send.at[step],
            shift_recv.at[step],
            z,
            to_chip,
            core,
        )

    def shift_start(step, carry):
        shift_copy(step, chip, wrap(chip + step, chips)).start()
        return carry

    lax.fori_loop(1, chips, shift_start, 0)

    def shift_wait(step, carry):
        shift_copy(step, wrap(chip - step, chips), chip).wait_recv()
        return carry

    loads[0].wait()
    loads[1].wait()
    pair[3].wait_recv()
    pair[4].wait_recv()
    lax.fori_loop(1, chips, shift_wait, 0)

    hidden = jnp.dot(shifted_all[...], wk_all[...], preferred_element_type=F32)
    act[...] = (jnp.maximum(hidden, 0.0) ** 2).astype(BF16)

    def sum_copy(source, to_chip):
        return remote(
            partial.at[to_chip],
            summed.at[source],
            sum_send.at[to_chip],
            sum_recv.at[source],
            z,
            to_chip,
            core,
        )

    def mix_out(step, carry):
        block = lax.rem(chip // 2 + 1 + step, chips // 2)
        cols = pl.ds(pl.multiple_of(block * 2 * LANES, 2 * LANES), 2 * LANES)
        part = jnp.dot(act[...], wv_all[:, cols], preferred_element_type=F32)
        partial[block * 2] = part[:, :LANES]
        partial[block * 2 + 1] = part[:, LANES:]
        for lower in range(2):
            to_chip = block * 2 + lower

            @pl.when(to_chip != chip)
            def _():
                sum_copy(chip, to_chip).start()

        return carry

    lax.fori_loop(0, chips // 2, mix_out, 0)

    def sum_in(step, total):
        source = wrap(chip + step, chips)
        sum_copy(source, chip).wait_recv()
        return total + summed[source]

    residual = lax.fori_loop(1, chips, sum_in, state + partial[chip])

    turned = residual.T
    stats[chip] = rows_of(
        jnp.sum(turned, axis=0, keepdims=True), jnp.sum(turned * turned, axis=0, keepdims=True)
    )

    def stat_copy(step, source, to_chip):
        return remote(
            stats.at[source],
            stats.at[source],
            stat_send.at[step],
            stat_recv.at[step],
            z,
            to_chip,
            core,
        )

    def stat_start(step, carry):
        stat_copy(step, chip, wrap(chip + step, chips)).start()
        return carry

    def stat_wait(step, carry):
        stat_copy(step, wrap(chip - step, chips), chip).wait_recv()
        return carry

    lax.fori_loop(1, chips, stat_start, 0)
    lax.fori_loop(1, chips, stat_wait, 0)
    total = jnp.sum(stats[...], axis=0)
    average = total[0:1] / width
    variance = total[1:2] / width - average * average
    scale = lax.rsqrt(variance + epsilon)
    model = core.astype(F32)
    gains = gain_ref[:, lane(chip)]
    biases = bias_ref[:, lane(chip)]
    gain = gains[0:1] * (1.0 - model) + gains[1:2] * model
    bias = biases[0:1] * (1.0 - model) + biases[1:2] * model
    normed = (residual - column_of(average)) * column_of(scale) * gain + bias
    place = z // side
    sets[0, place] = normed.astype(BF16)

    sends = []
    for step in range(1, per_set):
        copy = remote(
            sets.at[0, place],
            sets.at[0, place],
            set_send.at[step],
            set_recv.at[step],
            wrap(z + side * step, nz),
            chip,
            core,
        )
        copy.start()
        sends.append(copy)

    def head_wait(step, carry):
        head_copy(step).wait_recv()
        return carry

    keep.wait()
    lax.fori_loop(1, nz, head_wait, 0)
    stays = (
        pltpu.make_async_copy(
            head_own.at[:, 0:LANES], head_all.at[:, lane(x)], load_sem.at[4]
        ),
        pltpu.make_async_copy(
            head_own.at[:, LANES : 2 * LANES], head_all.at[:, lane(side + y)], load_sem.at[5]
        ),
    )
    for stay in stays:
        stay.start()
    spread = []
    for step in range(1, side):
        spread.append(
            remote(
                head_own.at[:, 0:LANES],
                head_all.at[:, lane(x)],
                hx_send.at[0, step],
                hx_recv.at[0, step],
                z,
                wrap(x + step, side) * side + y,
                core,
            )
        )
        spread.append(
            remote(
                head_own.at[:, LANES : 2 * LANES],
                head_all.at[:, lane(side + y)],
                hx_send.at[1, step],
                hx_recv.at[1, step],
                z,
                x * side + wrap(y + step, side),
                core,
            )
        )
    for copy in spread:
        copy.start()

    for copy in sends:
        copy.wait_recv()
    nears = []
    for slot, offset in enumerate(near):
        copy = remote(
            sets.at[0],
            sets.at[slot + 1],
            near_send.at[slot],
            near_recv.at[slot],
            wrap(z - sign * offset, nz),
            chip,
            core,
        )
        copy.start()
        nears.append(copy)

    def token_copy(slot, source, to_chip):
        return remote(
            sets.at[slot],
            tokens.at[:, :, lane(source)],
            tok_send.at[to_chip],
            tok_recv.at[source],
            z,
            to_chip,
            core,
        )

    for slot in range(side):
        if slot > 0:
            nears[slot - 1].wait_recv()
        offset = 0 if slot == 0 else near[slot - 1]
        group = lax.rem(wrap(z + sign * offset, nz), side)
        for to_x in range(side):
            to_chip = to_x * side + wrap(group - to_x, side)

            @pl.when(to_chip == chip)
            def _():
                tokens[:, :, lane(chip)] = sets[slot]

            @pl.when(to_chip != chip)
            def _():
                token_copy(slot, chip, to_chip).start()

    def target_wait(step, carry):
        remote(
            target_ref,
            targets_all.at[wrap(z - step, nz)],
            tgt_send.at[step],
            tgt_recv.at[step],
            z,
            chip,
            core,
        ).wait_recv()
        return carry

    lax.fori_loop(1, nz, target_wait, 0)
    wanted = jnp.concatenate(
        [
            column_of(targets_all[my_set + side * step][0:1].astype(F32))
            for step in range(per_set)
        ],
        axis=0,
    )

    for stay in stays:
        stay.wait()
    for copy in spread:
        copy.wait_recv()

    def token_wait(step, carry):
        source = wrap(chip + step, chips)
        token_copy(0, source, chip).wait_recv()
        return carry

    lax.fori_loop(1, chips, token_wait, 0)

    count = per_set * LANES

    def make_logits(block, peak):
        cols = pl.ds(pl.multiple_of(block * 2 * LANES, 2 * LANES), 2 * LANES)
        part = jnp.dot(
            tokens[...].reshape(count, width), head_all[:, cols], preferred_element_type=F32
        )
        logits[block] = part
        return jnp.maximum(peak, jnp.maximum(part[:, :LANES], part[:, LANES:]))

    peak = lax.fori_loop(0, side, make_logits, jnp.full((count, LANES), -jnp.inf, F32))
    peak = jnp.max(peak, axis=1, keepdims=True)
    total = jnp.zeros((count, LANES), F32)
    hit = jnp.zeros((count, LANES), F32)
    column = iota((count, LANES), 1).astype(F32)
    for block in range(side):
        for half in range(2):
            part = logits[block, :, half * LANES : (half + 1) * LANES]
            total = total + jnp.exp(part - peak)
            index = block * 2 + half
            if index < side:
                base = (index * side + y) * 2 * vocab_half + z * 2 * LANES
            else:
                base = (x * side + index - side) * 2 * vocab_half + z * 2 * LANES + LANES
            hit = hit + jnp.where(wanted - base.astype(F32) == column, part, 0.0)
    total = jnp.sum(total, axis=1, keepdims=True)
    hit = jnp.sum(hit, axis=1, keepdims=True)
    column = iota((count, LANES), 1)
    packed = jnp.where(column == 0, peak, jnp.where(column == 1, total, hit))
    for step in range(per_set):
        turned = packed[step * LANES : (step + 1) * LANES].T
        local_stats[step] = turned[0:8]

    def column_copy(step, source, to_z):
        return remote(
            local_stats.at[step],
            column_stats.at[source],
            c0_send.at[step],
            c0_recv.at[source],
            to_z,
            chip,
            core,
        )

    for step in range(per_set):
        to_z = my_set + side * step

        @pl.when(to_z == z)
        def _():
            column_stats[z] = local_stats[step]

        @pl.when(to_z != z)
        def _():
            column_copy(step, z, to_z).start()

    def combine(parts):
        peaks = parts[:, 0:1, :]
        top = jnp.max(peaks, axis=0)
        sums = jnp.sum(parts[:, 1:2, :] * jnp.exp(peaks - top[None]), axis=0)
        return top, sums, jnp.sum(parts[:, 2:3, :], axis=0)

    def plane_copy(step, source_x, to_chip):
        return remote(
            plane_stats.at[source_x],
            plane_stats.at[source_x],
            c1_send.at[step],
            c1_recv.at[source_x],
            z,
            to_chip,
            core,
        )

    @pl.when(my_set == z_set)
    def _():
        def column_wait(step, carry):
            source = wrap(z + step, nz)
            column_copy(0, source, z).wait_recv()
            return carry

        lax.fori_loop(1, nz, column_wait, 0)
        plane_stats[x] = rows_of(*combine(column_stats[...]))

        def plane_start(step, carry):
            plane_copy(step, x, wrap(chip + step, chips)).start()
            return carry

        lax.fori_loop(1, chips, plane_start, 0)

    for source_x in range(side):
        source = source_x * side + wrap(z_set - source_x, side)

        @pl.when(source != chip)
        def _():
            plane_copy(0, source_x, chip).wait_recv()

    top, sums, hits = combine(plane_stats[...])
    logp = hits - top - jnp.log(sums)
    logp_pair[0] = jnp.broadcast_to(logp, (8, LANES))
    swap = remote(
        logp_pair.at[0], logp_pair.at[1], pair_send.at[5], pair_recv.at[5], z, chip, other
    )
    swap.start()
    swap.wait_recv()
    own = logp_pair[0, 0:1]
    theirs = logp_pair[1, 0:1]
    policy = own * (1.0 - model) + theirs * model
    base_logp = own * model + theirs * (1.0 - model)
    length = (count_ref[z] - 1) * 64 + last_ref[z]
    valid = iota((1, LANES), 1) < length
    row = jnp.where(valid, policy, 0.0)
    ratio = jnp.sum(jnp.where(valid, policy - base_logp, 0.0), axis=1, keepdims=True)
    out_ref[...] = rows_of(row, jnp.broadcast_to(ratio, (1, LANES)))

    for copy in pair + (swap,):
        copy.wait_send()
    for copy in moves + picks + sends + nears + spread:
        copy.wait_send()

    def drain_z(step, carry):
        head_copy(step).wait_send()
        remote(
            target_ref,
            targets_all.at[z],
            tgt_send.at[step],
            tgt_recv.at[step],
            z,
            chip,
            core,
        ).wait_send()
        return carry

    lax.fori_loop(1, nz, drain_z, 0)

    def drain_plane(step, carry):
        to_chip = wrap(chip + step, chips)
        shift_copy(step, chip, to_chip).wait_send()
        stat_copy(step, chip, to_chip).wait_send()
        sum_copy(chip, to_chip).wait_send()
        token_copy(0, chip, to_chip).wait_send()
        return carry

    lax.fori_loop(1, chips, drain_plane, 0)
    for step in range(per_set):

        @pl.when(my_set + side * step != z)
        def _():
            column_copy(step, z, z).wait_send()

    @pl.when(my_set == z_set)
    def _():
        def drain_stats(step, carry):
            plane_copy(step, x, wrap(chip + step, chips)).wait_send()
            return carry

        lax.fori_loop(1, chips, drain_stats, 0)


def body(
    nz,
    side,
    pages,
    page_table,
    page_count,
    last_len,
    targets,
    mix_key,
    w_key,
    w_value,
    ln_gain,
    ln_bias,
    head,
):
    chips = side * side
    per_set = nz // side
    width = chips * LANES
    units = w_key.shape[2]
    rows = head.shape[1]
    tensor = lax.axis_index("tensor")
    core = tensor % 2
    low = core == 0

    def placed(value):
        zero = jnp.zeros_like(value)
        return jnp.concatenate(
            [jnp.where(low, value, zero), jnp.where(low, zero, value)], axis=-1
        )

    pages_wide = placed(pages)
    mix_wide = jnp.broadcast_to(placed(mix_key)[:, None, :], (2, 8, LANES))
    target_rows = jnp.broadcast_to(targets, (8, LANES))
    smem = pl.BlockSpec(memory_space=pltpu.SMEM)
    vmem = pl.BlockSpec(memory_space=pltpu.VMEM)
    hbm = pl.BlockSpec(memory_space=pl.ANY)
    dma = pltpu.SemaphoreType.DMA
    semaphores = [6, 6, 6]
    semaphores += [nz] * 2 + [4] * 2 + [per_set] * 2
    semaphores += [chips] * 6
    semaphores += [nz] * 2 + [(2, side)] * 2
    semaphores += [per_set] * 2 + [side] * 2 + [chips] * 2
    semaphores += [per_set, nz] + [chips, side]
    result = pl.pallas_call(
        functools.partial(kernel, nz, side),
        out_shape=jax.ShapeDtypeStruct((8, LANES), F32),
        in_specs=[smem] * 3 + [vmem] * 5 + [hbm] * 3,
        out_specs=vmem,
        scratch_shapes=[
            pltpu.VMEM((4, 64, LANES), BF16),
            pltpu.VMEM((8, LANES), F32),
            pltpu.VMEM((nz, 8, LANES), jnp.int32),
            pltpu.VMEM((2, rows, head.shape[2]), BF16),
            pltpu.VMEM((width, 2 * LANES), BF16),
            pltpu.VMEM((width, 2 * side * LANES), BF16),
            pltpu.VMEM((width, 2 * units), BF16),
            pltpu.VMEM((2 * units, width), BF16),
            pltpu.VMEM((side * 4, 64, LANES), BF16),
            pltpu.VMEM((per_set, 2, 64, LANES), BF16),
            pltpu.VMEM((per_set, 2, 64, LANES), BF16),
            pltpu.VMEM((LANES, width), BF16),
            pltpu.VMEM((LANES, 2 * units), BF16),
            pltpu.VMEM((chips, LANES, LANES), F32),
            pltpu.VMEM((chips, LANES, LANES), F32),
            pltpu.VMEM((chips, 8, LANES), F32),
            pltpu.VMEM((side, per_set, LANES, LANES), BF16),
            pltpu.VMEM((per_set, LANES, width), BF16),
            pltpu.VMEM((side, per_set * LANES, 2 * LANES), F32),
            pltpu.VMEM((per_set, 8, LANES), F32),
            pltpu.VMEM((nz, 8, LANES), F32),
            pltpu.VMEM((side, 8, LANES), F32),
            pltpu.VMEM((2, 8, LANES), F32),
        ]
        + [dma(size if isinstance(size, tuple) else (size,)) for size in semaphores],
        compiler_params=pltpu.CompilerParams(
            collective_id=0, has_side_effects=True, vmem_limit_bytes=48 * 1024 * 1024
        ),
    )(
        page_table,
        page_count,
        last_len,
        pages_wide,
        mix_wide,
        target_rows,
        ln_gain,
        ln_bias,
        w_key,
        w_value,
        head,
    )
    share = LANES // (2 * chips)
    token_part = lax.dynamic_slice(result, (0, tensor * share), (1, share))
    return token_part, result[1, 0:1]


def solution(mesh):
    nz = mesh.shape["dp"]
    side = {32: 4, 8: 2}[mesh.shape["tensor"]]
    specs = (
        P(None, "dp", None, "tensor"),
        P(),
        P(),
        P(),
        P("dp", None),
        P(None, "tensor"),
        P(None, None, "tensor"),
        P(None, "tensor", None),
        P(),
        P(),
        P(None, "dp", "tensor"),
    )
    return jax.shard_map(
        functools.partial(body, nz, side),
        mesh=mesh,
        in_specs=specs,
        out_specs=(P("dp", "tensor"), P("dp")),
        check_vma=False,
    )
```

```python
import functools

import jax
import jax.numpy as jnp
from jax import lax
from jax.experimental import pallas as pl
from jax.experimental.pallas import tpu as pltpu
from jax.sharding import PartitionSpec as P

epsilon = 1e-05
F32 = jnp.float32
BF16 = jnp.bfloat16
LANES = 128
BATCHES = {16: ((0, 8, 4, 12), (1, 15, 7, 9), (2, 14, 6, 10), (3, 13, 5, 11)), 4: ((0, 2), (1, 3))}
VMEM_LIMIT = 63 * 1024 * 1024


def iota(shape, axis):
    return lax.broadcasted_iota(jnp.int32, shape, axis)


def rows_of(*rows):
    place = iota((8, LANES), 0)
    tile = jnp.zeros((8, LANES), F32)
    for index, row in enumerate(rows):
        tile = jnp.where(place == index, jnp.broadcast_to(row, (8, LANES)), tile)
    return tile


def column_of(row):
    return jnp.broadcast_to(row, (LANES, LANES)).T


def kernel(
    nz,
    side,
    table_hbm,
    count_hbm,
    last_hbm,
    pages_hbm,
    mix_hbm,
    target_hbm,
    gain_hbm,
    bias_hbm,
    wk_hbm,
    wv_hbm,
    head_hbm,
    token_out,
    ratio_out,
    table_ref,
    count_ref,
    last_ref,
    pages_ref,
    mix_ref,
    gain_ref,
    bias_ref,
    pages_in,
    mix_in,
    targets_all,
    head_src,
    head_all,
    wk_all,
    wv_all,
    window,
    chosen,
    picked,
    shift_blocks,
    shifted_all,
    act,
    partial,
    line_sums,
    line_total,
    cross_sums,
    stats,
    sets,
    tokens,
    logits,
    local_stats,
    column_stats,
    plane_stats,
    pair_send,
    pair_recv,
    load_sem,
    tgt_send,
    tgt_recv,
    win_send,
    win_recv,
    pick_send,
    pick_recv,
    sa_send,
    sa_recv,
    sb_send,
    sb_recv,
    ra_send,
    ra_recv,
    rb_send,
    rb_recv,
    stat_send,
    stat_recv,
    hz_send,
    hz_recv,
    hf_send,
    hf_recv,
    hr_send,
    hr_recv,
    set_send,
    set_recv,
    near_send,
    near_recv,
    ta_send,
    ta_recv,
    tb_send,
    tb_recv,
    tr_send,
    tr_recv,
    c0_send,
    c0_recv,
    c1_send,
    c1_recv,
):
    chips = side * side
    per_set = nz // side
    z = lax.axis_index("dp")
    tensor = lax.axis_index("tensor")
    core = lax.rem(tensor, 2)
    other = 1 - core
    chip = tensor // 2
    x = chip // side
    y = lax.rem(chip, side)
    a = x * other + y * core
    b = y * other + x * core
    z_set = lax.rem(z, side)
    sign = 1 - 2 * core
    width = chips * LANES
    units = wk_hbm.shape[2]
    vocab_half = head_hbm.shape[2]
    rows = head_hbm.shape[1]
    slots = nz // 2
    near = {4: (1, -1, 2), 2: (1,)}[side]
    steps = (1, 3, 2) if side == 4 else (1,)
    ring = ((1, 0), (side - 1, 1)) if side == 4 else ((1, 0),)
    batches = BATCHES[nz]
    count = per_set * LANES

    def chip_at(at_a, at_b):
        return (at_a * side + at_b) * other + (at_b * side + at_a) * core

    def remote(src, dst, send, recv, to_z, to_chip, to_core):
        return pltpu.make_async_remote_copy(
            src_ref=src,
            dst_ref=dst,
            send_sem=send,
            recv_sem=recv,
            device_id={"dp": to_z, "tensor": to_chip * 2 + to_core},
            device_id_type=pl.DeviceIdType.MESH,
        )

    def await_bytes(view, sem):
        pltpu.make_async_copy(view, view, sem).wait()

    def wrap(value, size):
        return lax.rem(value + 4 * size, size)

    def lane(index):
        return pl.ds(pl.multiple_of(index * LANES, LANES), LANES)

    def pair_lane(index):
        return pl.ds(pl.multiple_of(index * 2 * LANES, 2 * LANES), 2 * LANES)

    def in_line(step):
        return chip_at(wrap(a + step, side), b)

    def across(step):
        return chip_at(a, wrap(b + step, side))

    unit_cols = pl.ds(pl.multiple_of(core * units, units), units)
    loads = (
        pltpu.make_async_copy(wk_hbm.at[core], wk_all.at[:, unit_cols], load_sem.at[0]),
        pltpu.make_async_copy(wv_hbm.at[core], wv_all.at[unit_cols, :], load_sem.at[1]),
        pltpu.make_async_copy(head_hbm.at[core], head_src.at[core], load_sem.at[2]),
    )
    small = (
        pltpu.make_async_copy(pages_hbm, pages_ref, load_sem.at[6]),
        pltpu.make_async_copy(mix_hbm, mix_ref, load_sem.at[7]),
        pltpu.make_async_copy(target_hbm, targets_all.at[z], load_sem.at[8]),
        pltpu.make_async_copy(gain_hbm, gain_ref, load_sem.at[9]),
        pltpu.make_async_copy(bias_hbm, bias_ref, load_sem.at[10]),
        pltpu.make_async_copy(table_hbm, table_ref, load_sem.at[11]),
        pltpu.make_async_copy(count_hbm, count_ref, load_sem.at[12]),
        pltpu.make_async_copy(last_hbm, last_ref, load_sem.at[13]),
    )
    for load in small + loads:
        load.start()

    barrier = pltpu.get_barrier_semaphore()

    def hello(to_z, to_chip, to_core):
        pl.semaphore_signal(
            barrier,
            inc=1,
            device_id={"dp": to_z, "tensor": to_chip * 2 + to_core},
            device_id_type=pl.DeviceIdType.MESH,
        )

    hello(z, chip, other)

    def hello_z(step, carry):
        hello(wrap(z + step, nz), chip, core)
        return carry

    def hello_plane(step, carry):
        hello(z, wrap(chip + step, chips), core)
        hello(z, wrap(chip + step, chips), other)
        return carry

    lax.fori_loop(1, nz, hello_z, 0)
    lax.fori_loop(1, chips, hello_plane, 0)
    for load in small:
        load.wait()
    pl.semaphore_wait(barrier, nz - 1 + 2 * (chips - 1) + 1)

    pair = (
        remote(pages_ref.at[other], pages_in, pair_send.at[0], pair_recv.at[0], z, chip, other),
        remote(mix_ref, mix_in, pair_send.at[1], pair_recv.at[1], z, chip, other),
        remote(
            head_hbm.at[other], head_src.at[core], pair_send.at[2], pair_recv.at[2], z, chip, other
        ),
        remote(
            wk_hbm.at[other],
            wk_all.at[:, unit_cols],
            pair_send.at[3],
            pair_recv.at[3],
            z,
            chip,
            other,
        ),
        remote(
            wv_hbm.at[other],
            wv_all.at[unit_cols, :],
            pair_send.at[4],
            pair_recv.at[4],
            z,
            chip,
            other,
        ),
    )
    for copy in pair:
        copy.start()

    pair[0].wait_recv()
    ours = pages_ref[core]
    theirs = pages_in[...]

    @pl.when(core == 0)
    def _():
        window[pl.ds(4, 4)] = jnp.concatenate([ours, theirs], axis=-1)

    @pl.when(core == 1)
    def _():
        window[pl.ds(4, 4)] = jnp.concatenate([theirs, ours], axis=-1)

    window_offsets = {4: (-1, 0, 1, 2), 2: (-1, 0)}[side]
    mine = window.at[pl.ds(4, 4)]
    moves = []
    for slot, offset in enumerate(window_offsets):
        if offset == 0:
            continue
        copy = remote(
            mine,
            window.at[pl.ds(slot * 4, 4)],
            win_send.at[slot],
            win_recv.at[slot],
            wrap(z - sign * offset, nz),
            chip,
            core,
        )
        copy.start()
        moves.append(copy)

    def head_row(index):
        place = (lax.rem(index, side) * side + index // side) * other + index * core
        return pl.ds(pl.multiple_of(place * rows, rows), rows)

    def head_piece(to_z):
        return head_src.at[to_z // slots, :, pair_lane(lax.rem(to_z, slots))]

    keep = pltpu.make_async_copy(
        head_piece(z), head_all.at[head_row(z), pair_lane(a)], load_sem.at[3]
    )

    def head_start(batch):
        for step in batches[batch]:
            if step == 0:
                keep.start()
                continue
            remote(
                head_piece(wrap(z + step, nz)),
                head_all.at[head_row(z), pair_lane(a)],
                hz_send,
                hz_recv.at[batch],
                wrap(z + step, nz),
                chip,
                core,
            ).start()

    def head_forward(batch):
        steps_in = batches[batch]
        if 0 in steps_in:
            keep.wait()
        arrived = len(steps_in) - (0 in steps_in)
        await_bytes(head_all.at[0 : arrived * rows, pair_lane(a)], hz_recv.at[batch])
        for step in steps_in:
            block = head_all.at[head_row(wrap(z - step, nz)), pair_lane(a)]
            for place, slot in ring:
                remote(
                    block, block, hf_send.at[slot], hf_recv.at[slot, batch], z, in_line(place), core
                ).start()

    def head_relay(batch):
        steps_in = batches[batch]
        for place, slot in ring:
            await_bytes(
                head_all.at[0 : len(steps_in) * rows, pair_lane(0)], hf_recv.at[slot, batch]
            )
        if side < 4:
            return
        for index, step in enumerate(steps_in):
            place, slot = ring[index % 2]
            source = wrap(a - place, side)
            block = head_all.at[head_row(wrap(z - step, nz)), pair_lane(source)]
            remote(
                block, block, hr_send, hr_recv.at[slot, batch], z, in_line(place), core
            ).start()

    for copy in moves:
        copy.wait_recv()

    picks = []
    for step in range(per_set):
        to_z = wrap(z + side * step, nz)
        for page in range(2):
            entry = table_ref[page, to_z]
            slot = lax.rem((entry // 4 - z) * sign + 1 + 4 * nz, nz)
            wanted = jnp.logical_and(slot < side, page < count_ref[to_z])
            flag = jnp.where(wanted, 1.0, 0.0).astype(F32)
            index = jnp.minimum(slot, side - 1) * 4 + lax.rem(entry, 4)
            block = (window[index].astype(F32) * flag).astype(BF16)
            if step == 0:
                picked[0, page] = block
            else:
                chosen[step, page] = block
        if step > 0:
            copy = remote(
                chosen.at[step],
                picked.at[step],
                pick_send.at[step],
                pick_recv.at[step],
                to_z,
                chip,
                core,
            )
            copy.start()
            picks.append(copy)

    loads[2].wait()
    pair[2].wait_recv()
    head_start(0)

    def send_target(step, carry):
        remote(
            targets_all.at[z],
            targets_all.at[z],
            tgt_send,
            tgt_recv,
            wrap(z + step, nz),
            chip,
            core,
        ).start()
        return carry

    lax.fori_loop(1, nz, send_target, 0)

    pair[1].wait_recv()
    for copy in picks:
        copy.wait_recv()
    state = picked[0].astype(F32)
    for step in range(1, per_set):
        state = state + picked[step].astype(F32)
    state = state.reshape(LANES, LANES)
    rolled = pltpu.roll(state, 1, 0)
    previous = jnp.where(iota((LANES, LANES), 0) == 0, 0.0, rolled)
    model = core.astype(F32)

    def of_model(pair_rows):
        return pair_rows[0:1] * (1.0 - model) + pair_rows[1:2] * model

    ours = of_model(mix_ref[...])
    theirs = of_model(mix_in[...])
    low = jnp.concatenate([ours, theirs], axis=-1)
    high = jnp.concatenate([theirs, ours], axis=-1)
    mix = low * (1.0 - model) + high * model
    shift_blocks[b, a] = (state + (previous - state) * mix).astype(BF16)

    line = []
    for index, step in enumerate(steps):
        block = shift_blocks.at[b, a]
        copy = remote(block, block, sa_send.at[index], sa_recv.at[index], z, in_line(step), core)
        copy.start()
        line.append(copy)
    head_start(1)
    for copy in line:
        copy.wait_recv()
    cross = []
    for index, step in enumerate(steps):
        block = shift_blocks.at[b]
        copy = remote(block, block, sb_send.at[index], sb_recv.at[index], z, across(step), core)
        copy.start()
        cross.append(copy)
    loads[0].wait()
    loads[1].wait()
    pair[3].wait_recv()
    pair[4].wait_recv()
    for copy in cross:
        copy.wait_recv()
    for at_b in range(side):
        for at_a in range(side):
            shifted_all[:, lane(chip_at(at_a, at_b))] = shift_blocks[at_b, at_a]

    hidden = jnp.dot(shifted_all[...], wk_all[...], preferred_element_type=F32)
    act[...] = (jnp.maximum(hidden, 0.0) ** 2).astype(BF16)
    sums = []
    for index, step in enumerate((side // 2,) + tuple(s for s in steps if s != side // 2) + (0,)):
        to_a = wrap(a + step, side)

        def mix_out(to_b, carry):
            cols = lane(chip_at(to_a, to_b))
            partial[to_a, to_b] = jnp.dot(
                act[...], wv_all[:, cols], preferred_element_type=F32
            )
            return carry

        lax.fori_loop(0, side, mix_out, 0)
        if step:
            copy = remote(
                partial.at[to_a],
                line_sums.at[step],
                ra_send.at[step],
                ra_recv.at[step],
                z,
                in_line(step),
                core,
            )
            copy.start()
            sums.append(copy)
    if len(batches) > 2:
        head_start(2)
    total = partial[a]
    for copy in sums:
        copy.wait_recv()
    for step in steps:
        total = total + line_sums[step]
    line_total[...] = total
    crosses = []
    for step in steps:
        copy = remote(
            line_total.at[wrap(b + step, side)],
            cross_sums.at[step],
            rb_send.at[step],
            rb_recv.at[step],
            z,
            across(step),
            core,
        )
        copy.start()
        crosses.append(copy)
    if len(batches) > 2:
        head_start(3)
    residual = state + line_total[b]
    for step, copy in zip(steps, crosses):
        copy.wait_recv()
    for step in steps:
        residual = residual + cross_sums[step]

    turned = residual.T
    stats[chip] = rows_of(
        jnp.sum(turned, axis=0, keepdims=True), jnp.sum(turned * turned, axis=0, keepdims=True)
    )

    def stat_start(step, carry):
        remote(
            stats.at[chip],
            stats.at[chip],
            stat_send,
            stat_recv,
            z,
            wrap(chip + step, chips),
            core,
        ).start()
        return carry

    lax.fori_loop(1, chips, stat_start, 0)
    head_forward(0)
    await_bytes(stats.at[pl.ds(0, chips - 1)], stat_recv)
    total = jnp.sum(stats[...], axis=0)
    average = total[0:1] / width
    variance = total[1:2] / width - average * average
    scale = lax.rsqrt(variance + epsilon)
    gain = of_model(gain_ref[:, lane(chip)])
    bias = of_model(bias_ref[:, lane(chip)])
    normed = (residual - column_of(average)) * column_of(scale) * gain + bias
    place = z // side
    sets[0, place] = normed.astype(BF16)

    sends = []
    for step in range(1, per_set):
        copy = remote(
            sets.at[0, place],
            sets.at[0, place],
            set_send.at[step],
            set_recv.at[step],
            wrap(z + side * step, nz),
            chip,
            core,
        )
        copy.start()
        sends.append(copy)
    head_forward(1)
    head_relay(0)

    for copy in sends:
        copy.wait_recv()
    nears = []
    for slot, offset in enumerate(near):
        copy = remote(
            sets.at[0],
            sets.at[slot + 1],
            near_send.at[slot],
            near_recv.at[slot],
            wrap(z - sign * offset, nz),
            chip,
            core,
        )
        copy.start()
        nears.append(copy)

    def token_cols(at_b, at_a):
        return lane(at_b * side + at_a)

    for slot in range(side):
        if slot > 0:
            nears[slot - 1].wait_recv()
        offset = 0 if slot == 0 else near[slot - 1]
        group = lax.rem(wrap(z + sign * offset, nz), side)

        @pl.when(group == a)
        def _():
            tokens[:, :, token_cols(b, a)] = sets[slot]

        @pl.when(group != a)
        def _():
            remote(
                sets.at[slot],
                tokens.at[:, :, token_cols(b, a)],
                ta_send,
                ta_recv,
                z,
                chip_at(group, b),
                core,
            ).start()

        if slot == 0:
            if len(batches) > 2:
                head_forward(2)
            head_relay(1)

    await_bytes(targets_all.at[pl.ds(0, nz - 1)], tgt_recv)
    wanted = jnp.concatenate(
        [
            column_of(targets_all[a + side * step].astype(F32))
            for step in range(per_set)
        ],
        axis=0,
    )

    if len(batches) > 2:
        head_forward(3)
        head_relay(2)

    def token_block(at_b, first, size):
        start = pl.multiple_of((at_b * side + first) * LANES, LANES)
        return tokens.at[:, :, pl.ds(start, size * LANES)]

    await_bytes(tokens.at[:, :, pl.ds(0, (side - 1) * LANES)], ta_recv)
    for place, slot in ring:
        block = token_block(b, 0, side)
        remote(block, block, tb_send.at[slot], tb_recv.at[slot], z, across(place), core).start()
    if len(batches) > 2:
        head_relay(3)
    for place, slot in ring:
        await_bytes(token_block(0, 0, side), tb_recv.at[slot])
        if side == 4:
            block = token_block(wrap(b - place, side), 2 * slot, 2)
            remote(block, block, tr_send, tr_recv.at[slot], z, across(place), core).start()
    if side == 4:
        for place, slot in ring:
            for batch, steps_in in enumerate(batches):
                await_bytes(
                    head_all.at[0 : len(steps_in) // 2 * rows, pair_lane(0)],
                    hr_recv.at[slot, batch],
                )
        for place, slot in ring:
            await_bytes(token_block(0, 0, 2), tr_recv.at[slot])

    def make_logits(block, peak):
        part = jnp.dot(
            tokens[...].reshape(count, width),
            head_all[:, pair_lane(block)],
            preferred_element_type=F32,
        )
        logits[block] = part
        return jnp.maximum(peak, jnp.maximum(part[:, :LANES], part[:, LANES:]))

    peak = lax.fori_loop(0, side, make_logits, jnp.full((count, LANES), -jnp.inf, F32))
    peak = jnp.max(peak, axis=1, keepdims=True)
    total = jnp.zeros((count, LANES), F32)
    hit = jnp.zeros((count, LANES), F32)
    column = iota((count, LANES), 1).astype(F32)
    for block in range(side):
        for half in range(2):
            part = logits[block, :, half * LANES : (half + 1) * LANES]
            total = total + jnp.exp(part - peak)
            base = chip_at(block, b) * 2 * vocab_half + (z * 2 + half) * LANES
            hit = hit + jnp.where(wanted - base.astype(F32) == column, part, 0.0)
    total = jnp.sum(total, axis=1, keepdims=True)
    hit = jnp.sum(hit, axis=1, keepdims=True)
    column = iota((count, LANES), 1)
    packed = jnp.where(column == 0, peak, jnp.where(column == 1, total, hit))
    for step in range(per_set):
        turned = packed[step * LANES : (step + 1) * LANES].T
        local_stats[step] = turned[0:8]

    for step in range(per_set):
        to_z = a + side * step

        @pl.when(to_z == z)
        def _():
            column_stats[z] = local_stats[step]

        @pl.when(to_z != z)
        def _():
            remote(
                local_stats.at[step], column_stats.at[z], c0_send.at[step], c0_recv, to_z, chip, core
            ).start()

    def combine(parts):
        peaks = parts[:, 0:1, :]
        top = jnp.max(peaks, axis=0)
        sums = jnp.sum(parts[:, 1:2, :] * jnp.exp(peaks - top[None]), axis=0)
        return top, sums, jnp.sum(parts[:, 2:3, :], axis=0)

    mine = plane_stats.at[core, b]

    @pl.when(a == z_set)
    def _():
        await_bytes(column_stats.at[pl.ds(0, nz - 1)], c0_recv)
        plane_stats[core, b] = rows_of(*combine(column_stats[...]))

        def plane_start(step, carry):
            to_chip = wrap(chip + step, chips)
            remote(mine, mine, c1_send.at[0], c1_recv.at[core, b], z, to_chip, core).start()
            remote(mine, mine, c1_send.at[1], c1_recv.at[core, b], z, to_chip, other).start()
            return carry

        remote(mine, mine, c1_send.at[1], c1_recv.at[core, b], z, chip, other).start()
        lax.fori_loop(1, chips, plane_start, 0)

    for of_core in range(2):
        for at_b in range(side):
            theirs = plane_stats.at[of_core, at_b]
            ours = jnp.logical_and(
                jnp.logical_and(core == of_core, b == at_b), a == z_set
            )

            @pl.when(jnp.logical_not(ours))
            def _():
                await_bytes(theirs, c1_recv.at[of_core, at_b])

    logp = []
    for of_core in range(2):
        top, sums_all, hits = combine(plane_stats[of_core])
        logp.append(hits - top - jnp.log(sums_all))
    length = (count_ref[z] - 1) * 64 + last_ref[z]
    valid = iota((1, LANES), 1) < length
    row = jnp.where(valid, logp[0], 0.0)
    ratio_out[...] = jnp.sum(
        jnp.where(valid, logp[0] - logp[1], 0.0), axis=1, keepdims=True
    )
    share = token_out.shape[1]
    row = pltpu.roll(jnp.broadcast_to(row, (8, LANES)), lax.rem(LANES - tensor * share, LANES), 1)
    token_out[...] = row[0:1, 0:share]

    for copy in pair:
        copy.wait_send()
    for copy in moves + picks + line + cross + sums + crosses + sends + nears:
        copy.wait_send()
    await_bytes(targets_all.at[pl.ds(0, nz - 1)], tgt_send)
    await_bytes(stats.at[pl.ds(0, chips - 1)], stat_send)
    await_bytes(head_all.at[0 : (nz - 1) * rows, pair_lane(0)], hz_send)
    for place, slot in ring:
        await_bytes(head_all.at[:, pair_lane(0)], hf_send.at[slot])
        await_bytes(token_block(0, 0, side), tb_send.at[slot])
    await_bytes(tokens.at[:, :, pl.ds(0, (side - 1) * LANES)], ta_send)
    if side == 4:
        await_bytes(head_all.at[:, pair_lane(0)], hr_send)
        await_bytes(token_block(0, 0, side), tr_send)
    for step in range(per_set):

        @pl.when(a + side * step != z)
        def _():
            await_bytes(local_stats.at[step], c0_send.at[step])

    @pl.when(a == z_set)
    def _():
        await_bytes(stats.at[pl.ds(0, chips - 1)], c1_send.at[0])
        await_bytes(stats, c1_send.at[1])


def body(
    nz,
    side,
    pages,
    page_table,
    page_count,
    last_len,
    targets,
    mix_key,
    w_key,
    w_value,
    ln_gain,
    ln_bias,
    head,
):
    chips = side * side
    per_set = nz // side
    width = chips * LANES
    units = w_key.shape[2]
    rows = head.shape[1]
    vmem = pl.BlockSpec(memory_space=pltpu.VMEM)
    hbm = pl.BlockSpec(memory_space=pl.ANY)
    dma = pltpu.SemaphoreType.DMA
    batches = len(BATCHES[nz])
    share = LANES // (2 * chips)
    semaphores = [6, 6, 14, (), ()]
    semaphores += [4] * 2 + [per_set] * 2 + [side] * 8
    semaphores += [(), (), (), batches, 2, (2, batches), (), (2, batches)]
    semaphores += [per_set] * 2 + [side] * 2 + [(), (), 2, 2, (), 2]
    semaphores += [per_set, (), 2, (2, side)]
    result = pl.pallas_call(
        functools.partial(kernel, nz, side),
        out_shape=(
            jax.ShapeDtypeStruct((1, share), F32),
            jax.ShapeDtypeStruct((1, 1), F32),
        ),
        in_specs=[hbm] * 11,
        out_specs=(vmem, vmem),
        scratch_shapes=[
            pltpu.SMEM(page_table.shape[::-1], jnp.int32),
            pltpu.SMEM(page_count.shape, jnp.int32),
            pltpu.SMEM(last_len.shape, jnp.int32),
            pltpu.VMEM(pages.shape, BF16),
            pltpu.VMEM(mix_key.shape, F32),
            pltpu.VMEM(ln_gain.shape, F32),
            pltpu.VMEM(ln_bias.shape, F32),
            pltpu.VMEM(pages.shape[1:], BF16),
            pltpu.VMEM(mix_key.shape, F32),
            pltpu.VMEM((nz, 1, LANES), jnp.int32),
            pltpu.VMEM((2, rows, head.shape[2]), BF16),
            pltpu.VMEM((width, 2 * side * LANES), BF16),
            pltpu.VMEM((width, 2 * units), BF16),
            pltpu.VMEM((2 * units, width), BF16),
            pltpu.VMEM((side * 4, 64, LANES), BF16),
            pltpu.VMEM((per_set, 2, 64, LANES), BF16),
            pltpu.VMEM((per_set, 2, 64, LANES), BF16),
            pltpu.VMEM((side, side, LANES, LANES), BF16),
            pltpu.VMEM((LANES, width), BF16),
            pltpu.VMEM((LANES, 2 * units), BF16),
            pltpu.VMEM((side, side, LANES, LANES), F32),
            pltpu.VMEM((side, side, LANES, LANES), F32),
            pltpu.VMEM((side, LANES, LANES), F32),
            pltpu.VMEM((side, LANES, LANES), F32),
            pltpu.VMEM((chips, 8, LANES), F32),
            pltpu.VMEM((side, per_set, LANES, LANES), BF16),
            pltpu.VMEM((per_set, LANES, width), BF16),
            pltpu.VMEM((side, per_set * LANES, 2 * LANES), F32),
            pltpu.VMEM((per_set, 8, LANES), F32),
            pltpu.VMEM((nz, 8, LANES), F32),
            pltpu.VMEM((2, side, 8, LANES), F32),
        ]
        + [dma(size if isinstance(size, tuple) else (size,)) for size in semaphores],
        compiler_params=pltpu.CompilerParams(
            collective_id=0, has_side_effects=True, vmem_limit_bytes=VMEM_LIMIT
        ),
    )(
        page_table.T,
        page_count,
        last_len,
        pages,
        mix_key,
        targets,
        ln_gain,
        ln_bias,
        w_key,
        w_value,
        head,
    )
    token_part, ratio = result
    return token_part, ratio.reshape(1)


def solution(mesh):
    nz = mesh.shape["dp"]
    side = {32: 4, 8: 2}[mesh.shape["tensor"]]
    specs = (
        P(None, "dp", None, "tensor"),
        P(),
        P(),
        P(),
        P("dp", None),
        P(None, "tensor"),
        P(None, None, "tensor"),
        P(None, "tensor", None),
        P(),
        P(),
        P(None, "dp", "tensor"),
    )
    return jax.shard_map(
        functools.partial(body, nz, side),
        mesh=mesh,
        in_specs=specs,
        out_specs=(P("dp", "tensor"), P("dp")),
        check_vma=False,
    )
```

```python
import functools

import jax
import jax.numpy as jnp
from jax import lax
from jax.experimental import pallas as pl
from jax.experimental.pallas import tpu as pltpu
from jax.sharding import PartitionSpec as P

epsilon = 1e-05
F32 = jnp.float32
BF16 = jnp.bfloat16
LANES = 128
BATCHES = {16: ((0, 8, 4, 12), (1, 15, 7, 9), (2, 14, 6, 10), (3, 13, 5, 11)), 4: ((0, 2), (1, 3))}
VMEM_LIMIT = 63 * 1024 * 1024


ORDER = {4: (0, 1, 3, 2), 2: (0, 1)}
PARTS = {4: ((0, 3, (1, 3)), (3, 1, (2,))), 2: ((0, 1, ()), (1, 1, (1,)))}
SCHEDULE = {
    1: (("s", 0), ("s", 1)),
    2: (("s", 2),),
    4: (("s", 3),),
    5: (("f", 0),),
    6: (("f", 1), ("r", 0)),
    7: (("f", 2), ("r", 1)),
    9: (("f", 3), ("r", 2)),
    10: (("r", 3),),
}


def iota(shape, axis):
    return lax.broadcasted_iota(jnp.int32, shape, axis)


def rows_of(*rows):
    place = iota((8, LANES), 0)
    tile = jnp.zeros((8, LANES), F32)
    for index, row in enumerate(rows):
        tile = jnp.where(place == index, jnp.broadcast_to(row, (8, LANES)), tile)
    return tile


def column_of(row):
    return jnp.broadcast_to(row, (LANES, LANES)).T


def kernel(
    nz,
    side,
    table_hbm,
    count_hbm,
    last_hbm,
    pages_hbm,
    mix_hbm,
    target_hbm,
    gain_hbm,
    bias_hbm,
    wk_hbm,
    wv_hbm,
    head_hbm,
    out_ref,
    table_ref,
    count_ref,
    last_ref,
    pages_ref,
    mix_ref,
    gain_ref,
    bias_ref,
    pages_in,
    mix_in,
    targets_all,
    head_src,
    head_all,
    wk_all,
    wv_all,
    window,
    chosen,
    picked,
    shift_blocks,
    shifted_all,
    act,
    partial,
    line_sums,
    line_total,
    cross_sums,
    stats,
    sets,
    tokens,
    logits,
    local_stats,
    column_stats,
    plane_stats,
    pair_send,
    pair_recv,
    load_sem,
    tgt_send,
    tgt_recv,
    win_send,
    win_recv,
    pick_send,
    pick_recv,
    sa_send,
    sa_recv,
    sb_send,
    sb_recv,
    ra_send,
    ra_recv,
    rb_send,
    rb_recv,
    stat_send,
    stat_recv,
    hz_send,
    hz_recv,
    hf_send,
    hf_recv,
    hr_send,
    hr_recv,
    set_send,
    set_recv,
    ta_send,
    ta_recv,
    tb_send,
    tb_recv,
    tr_send,
    tr_recv,
    c0_send,
    c0_recv,
    c1_send,
    c1_recv,
):
    chips = side * side
    per_set = nz // side
    z = lax.axis_index("dp")
    tensor = lax.axis_index("tensor")
    core = lax.rem(tensor, 2)
    other = 1 - core
    chip = tensor // 2
    x = chip // side
    y = lax.rem(chip, side)
    a = x * other + y * core
    b = y * other + x * core
    z_set = lax.rem(z, side)
    sign = 1 - 2 * core
    width = chips * LANES
    units = wk_hbm.shape[2]
    vocab_half = head_hbm.shape[2]
    rows = head_hbm.shape[1]
    slots = nz // 2
    near = {4: (1, -1, 2), 2: (1,)}[side]
    steps = (1, 3, 2) if side == 4 else (1,)
    ring = ((1, 0), (side - 1, 1)) if side == 4 else ((1, 0),)
    batches = BATCHES[nz]
    count = per_set * LANES
    order = ORDER[per_set]
    parts = PARTS[per_set]

    def wrap(value, size):
        return lax.rem(value + 4 * size, size)

    gap = wrap(a - z_set, side)
    if side == 4:
        gap = gap - 4 * (gap // 3) + 2 * (sign - 1) * (gap // 2 - gap // 3)
    else:
        gap = gap * sign
    from_z = wrap(z + gap, nz)

    def chip_at(at_a, at_b):
        return (at_a * side + at_b) * other + (at_b * side + at_a) * core

    def remote(src, dst, send, recv, to_z, to_chip, to_core):
        return pltpu.make_async_remote_copy(
            src_ref=src,
            dst_ref=dst,
            send_sem=send,
            recv_sem=recv,
            device_id={"dp": to_z, "tensor": to_chip * 2 + to_core},
            device_id_type=pl.DeviceIdType.MESH,
        )

    def await_bytes(view, sem):
        pltpu.make_async_copy(view, view, sem).wait()

    def lane(index):
        return pl.ds(pl.multiple_of(index * LANES, LANES), LANES)

    def pair_lane(index):
        return pl.ds(pl.multiple_of(index * 2 * LANES, 2 * LANES), 2 * LANES)

    def in_line(step):
        return chip_at(wrap(a + step, side), b)

    def across(step):
        return chip_at(a, wrap(b + step, side))

    unit_cols = pl.ds(pl.multiple_of(core * units, units), units)
    loads = (
        pltpu.make_async_copy(wk_hbm.at[core], wk_all.at[:, unit_cols], load_sem.at[0]),
        pltpu.make_async_copy(wv_hbm.at[core], wv_all.at[unit_cols, :], load_sem.at[1]),
        pltpu.make_async_copy(head_hbm.at[core], head_src.at[core], load_sem.at[2]),
    )
    small = (
        pltpu.make_async_copy(pages_hbm, pages_ref, load_sem.at[6]),
        pltpu.make_async_copy(mix_hbm, mix_ref, load_sem.at[7]),
        pltpu.make_async_copy(target_hbm, targets_all.at[z], load_sem.at[8]),
        pltpu.make_async_copy(gain_hbm, gain_ref, load_sem.at[9]),
        pltpu.make_async_copy(bias_hbm, bias_ref, load_sem.at[10]),
        pltpu.make_async_copy(table_hbm, table_ref, load_sem.at[11]),
        pltpu.make_async_copy(count_hbm, count_ref, load_sem.at[12]),
        pltpu.make_async_copy(last_hbm, last_ref, load_sem.at[13]),
    )
    for load in small + loads:
        load.start()

    barrier = pltpu.get_barrier_semaphore()

    def hello(to_z, to_chip, to_core):
        pl.semaphore_signal(
            barrier,
            inc=1,
            device_id={"dp": to_z, "tensor": to_chip * 2 + to_core},
            device_id_type=pl.DeviceIdType.MESH,
        )

    hello(z, chip, other)

    def hello_z(step, carry):
        hello(wrap(z + step, nz), chip, core)
        return carry

    def hello_plane(step, carry):
        hello(z, wrap(chip + step, chips), core)
        hello(z, wrap(chip + step, chips), other)
        return carry

    @pl.when(gap != 0)
    def _():
        for at_a in range(side):
            hello(from_z, chip_at(at_a, b), core)

    lax.fori_loop(1, nz, hello_z, 0)
    lax.fori_loop(1, chips, hello_plane, 0)
    for load in small:
        load.wait()
    pl.semaphore_wait(barrier, nz - 1 + 2 * (chips - 1) + 1 + len(near))

    pair = (
        remote(pages_ref.at[other], pages_in, pair_send.at[0], pair_recv.at[0], z, chip, other),
        remote(mix_ref, mix_in, pair_send.at[1], pair_recv.at[1], z, chip, other),
        remote(
            head_hbm.at[other], head_src.at[core], pair_send.at[2], pair_recv.at[2], z, chip, other
        ),
        remote(
            wk_hbm.at[other],
            wk_all.at[:, unit_cols],
            pair_send.at[3],
            pair_recv.at[3],
            z,
            chip,
            other,
        ),
        remote(
            wv_hbm.at[other],
            wv_all.at[unit_cols, :],
            pair_send.at[4],
            pair_recv.at[4],
            z,
            chip,
            other,
        ),
    )
    for copy in pair:
        copy.start()

    def head_row(index):
        place = (lax.rem(index, side) * side + index // side) * other + index * core
        return pl.ds(pl.multiple_of(place * rows, rows), rows)

    def head_piece(to_z):
        return head_src.at[to_z // slots, :, pair_lane(lax.rem(to_z, slots))]

    keep = pltpu.make_async_copy(
        head_piece(z), head_all.at[head_row(z), pair_lane(a)], load_sem.at[3]
    )

    def head_start(batch):
        for step in batches[batch]:
            if step == 0:
                keep.start()
                continue
            remote(
                head_piece(wrap(z + step, nz)),
                head_all.at[head_row(z), pair_lane(a)],
                hz_send,
                hz_recv.at[batch],
                wrap(z + step, nz),
                chip,
                core,
            ).start()

    def head_forward(batch):
        steps_in = batches[batch]
        if 0 in steps_in:
            keep.wait()
        arrived = len(steps_in) - (0 in steps_in)
        await_bytes(head_all.at[0 : arrived * rows, pair_lane(a)], hz_recv.at[batch])
        for step in steps_in:
            block = head_all.at[head_row(wrap(z - step, nz)), pair_lane(a)]
            for place, slot in ring:
                remote(
                    block, block, hf_send.at[slot], hf_recv.at[slot, batch], z, in_line(place), core
                ).start()

    def head_relay(batch):
        steps_in = batches[batch]
        for place, slot in ring:
            await_bytes(
                head_all.at[0 : len(steps_in) * rows, pair_lane(0)], hf_recv.at[slot, batch]
            )
        if side < 4:
            return
        for index, step in enumerate(steps_in):
            place, slot = ring[index % 2]
            source = wrap(a - place, side)
            block = head_all.at[head_row(wrap(z - step, nz)), pair_lane(source)]
            remote(
                block, block, hr_send, hr_recv.at[slot, batch], z, in_line(place), core
            ).start()

    def at(point):
        for action, batch in SCHEDULE.get(point, ()):
            if batch >= len(batches):
                continue
            if (action, batch) == ("s", 0):
                loads[2].wait()
                pair[2].wait_recv()
            {"s": head_start, "f": head_forward, "r": head_relay}[action](batch)

    pair[0].wait_recv()
    ours = pages_ref[core]
    theirs = pages_in[...]

    @pl.when(core == 0)
    def _():
        window[pl.ds(4, 4)] = jnp.concatenate([ours, theirs], axis=-1)

    @pl.when(core == 1)
    def _():
        window[pl.ds(4, 4)] = jnp.concatenate([theirs, ours], axis=-1)

    window_offsets = {4: (-1, 0, 1, 2), 2: (-1, 0)}[side]
    mine = window.at[pl.ds(4, 4)]
    moves = []
    for slot, offset in enumerate(window_offsets):
        if offset == 0:
            continue
        copy = remote(
            mine,
            window.at[pl.ds(slot * 4, 4)],
            win_send.at[slot],
            win_recv.at[slot],
            wrap(z - sign * offset, nz),
            chip,
            core,
        )
        copy.start()
        moves.append(copy)

    at(0)
    for copy in moves:
        copy.wait_recv()

    picks = []
    for step in range(per_set):
        to_z = wrap(z + side * step, nz)
        for page in range(2):
            entry = table_ref[page, to_z]
            slot = lax.rem((entry // 4 - z) * sign + 1 + 4 * nz, nz)
            wanted = jnp.logical_and(slot < side, page < count_ref[to_z])
            flag = jnp.where(wanted, 1.0, 0.0).astype(F32)
            index = jnp.minimum(slot, side - 1) * 4 + lax.rem(entry, 4)
            block = (window[index].astype(F32) * flag).astype(BF16)
            if step == 0:
                picked[0, page] = block
            else:
                chosen[step, page] = block
        if step > 0:
            copy = remote(
                chosen.at[step],
                picked.at[step],
                pick_send.at[step],
                pick_recv.at[step],
                to_z,
                chip,
                core,
            )
            copy.start()
            picks.append(copy)

    at(1)

    def send_target(step, carry):
        remote(
            targets_all.at[z],
            targets_all.at[z],
            tgt_send,
            tgt_recv,
            wrap(z + step, nz),
            chip,
            core,
        ).start()
        return carry

    lax.fori_loop(1, nz, send_target, 0)

    pair[1].wait_recv()
    for copy in picks:
        copy.wait_recv()
    state = picked[0].astype(F32)
    for step in range(1, per_set):
        state = state + picked[step].astype(F32)
    state = state.reshape(LANES, LANES)
    rolled = pltpu.roll(state, 1, 0)
    previous = jnp.where(iota((LANES, LANES), 0) == 0, 0.0, rolled)
    model = core.astype(F32)

    def of_model(pair_rows):
        return pair_rows[0:1] * (1.0 - model) + pair_rows[1:2] * model

    ours = of_model(mix_ref[...])
    theirs = of_model(mix_in[...])
    low = jnp.concatenate([ours, theirs], axis=-1)
    high = jnp.concatenate([theirs, ours], axis=-1)
    mix = low * (1.0 - model) + high * model
    shift_blocks[b, a] = (state + (previous - state) * mix).astype(BF16)

    line = []
    for index, step in enumerate(steps):
        block = shift_blocks.at[b, a]
        copy = remote(block, block, sa_send.at[index], sa_recv.at[index], z, in_line(step), core)
        copy.start()
        line.append(copy)
    at(2)
    for copy in line:
        copy.wait_recv()
    cross = []
    for index, step in enumerate(steps):
        block = shift_blocks.at[b]
        copy = remote(block, block, sb_send.at[index], sb_recv.at[index], z, across(step), core)
        copy.start()
        cross.append(copy)
    at(3)
    loads[0].wait()
    loads[1].wait()
    pair[3].wait_recv()
    pair[4].wait_recv()
    for copy in cross:
        copy.wait_recv()
    for at_b in range(side):
        for at_a in range(side):
            shifted_all[:, lane(chip_at(at_a, at_b))] = shift_blocks[at_b, at_a]

    hidden = jnp.dot(shifted_all[...], wk_all[...], preferred_element_type=F32)
    act[...] = (jnp.maximum(hidden, 0.0) ** 2).astype(BF16)
    sums = []
    for index, step in enumerate((side // 2,) + tuple(s for s in steps if s != side // 2) + (0,)):
        to_a = wrap(a + step, side)

        def mix_out(to_b, carry):
            cols = lane(chip_at(to_a, to_b))
            partial[to_a, to_b] = jnp.dot(
                act[...], wv_all[:, cols], preferred_element_type=F32
            )
            return carry

        lax.fori_loop(0, side, mix_out, 0)
        if step:
            copy = remote(
                partial.at[to_a],
                line_sums.at[step],
                ra_send.at[step],
                ra_recv.at[step],
                z,
                in_line(step),
                core,
            )
            copy.start()
            sums.append(copy)
    at(4)
    total = partial[a]
    for copy in sums:
        copy.wait_recv()
    for step in steps:
        total = total + line_sums[step]
    line_total[...] = total
    crosses = []
    for step in steps:
        copy = remote(
            line_total.at[wrap(b + step, side)],
            cross_sums.at[step],
            rb_send.at[step],
            rb_recv.at[step],
            z,
            across(step),
            core,
        )
        copy.start()
        crosses.append(copy)
    at(5)
    residual = state + line_total[b]
    for step, copy in zip(steps, crosses):
        copy.wait_recv()
    for step in steps:
        residual = residual + cross_sums[step]

    turned = residual.T
    stats[chip] = rows_of(
        jnp.sum(turned, axis=0, keepdims=True), jnp.sum(turned * turned, axis=0, keepdims=True)
    )

    def stat_start(step, carry):
        remote(
            stats.at[chip],
            stats.at[chip],
            stat_send,
            stat_recv,
            z,
            wrap(chip + step, chips),
            core,
        ).start()
        return carry

    lax.fori_loop(1, chips, stat_start, 0)
    at(6)
    await_bytes(stats.at[pl.ds(0, chips - 1)], stat_recv)
    total = jnp.sum(stats[...], axis=0)
    average = total[0:1] / width
    variance = total[1:2] / width - average * average
    scale = lax.rsqrt(variance + epsilon)
    gain = of_model(gain_ref[:, lane(chip)])
    bias = of_model(bias_ref[:, lane(chip)])
    normed = (residual - column_of(average)) * column_of(scale) * gain + bias
    sets[0] = normed.astype(BF16)

    sends = {}
    for step in range(1, per_set):
        slot = order.index(per_set - step)
        sends[step] = remote(
            sets.at[0],
            sets.at[slot],
            set_send.at[step],
            set_recv.at[step],
            wrap(z + side * step, nz),
            chip,
            core,
        )
        sends[step].start()
    at(7)

    def token_cols(at_b, at_a):
        return lane(at_b * side + at_a)

    def token_copy(first, size, at_a, to_z):
        return remote(
            sets.at[pl.ds(first, size)],
            tokens.at[pl.ds(first, size), :, token_cols(b, at_a)],
            ta_send,
            ta_recv.at[at_a],
            to_z,
            chip_at(z_set, b),
            core,
        )

    for index, (first, size, needs) in enumerate(parts):
        for step in needs:
            sends[step].wait_recv()
        for offset in reversed((0,) + near):
            if offset:
                token_copy(first, size, a, wrap(z - sign * offset, nz)).start()
                continue

            @pl.when(gap == 0)
            def _():
                tokens[first : first + size, :, token_cols(b, a)] = sets[first : first + size]

            @pl.when(gap != 0)
            def _():
                token_copy(first, size, a, z).start()

        at(8 + index)

    await_bytes(targets_all.at[pl.ds(0, nz - 1)], tgt_recv)
    rollouts = [wrap(from_z + side * step, nz) for step in order]
    wanted = jnp.concatenate(
        [column_of(targets_all[rollout].astype(F32)) for rollout in rollouts], axis=0
    )

    half = side // 2

    def token_block(at_b, first, size):
        start = pl.multiple_of((at_b * side + first) * LANES, LANES)
        return tokens.at[:, :, pl.ds(start, size * LANES)]

    for at_a in range(side):

        @pl.when(jnp.logical_not(jnp.logical_and(gap == 0, a == at_a)))
        def _():
            await_bytes(tokens.at[:, :, pl.ds(0, LANES)], ta_recv.at[at_a])

    for turn in range(2):
        for place, slot in ring:
            part = (turn + slot) % 2
            block = token_block(b, part * half, half)
            remote(
                block, block, tb_send.at[slot], tb_recv.at[slot, turn], z, across(place), core
            ).start()
    at(10)
    if side == 4:
        for place, slot in ring:
            await_bytes(token_block(0, 0, half), tb_recv.at[slot, 0])
            block = token_block(wrap(b - place, side), slot * half, half)
            remote(block, block, tr_send, tr_recv.at[slot], z, across(place), core).start()
    else:
        await_bytes(token_block(0, 0, half), tb_recv.at[0, 0])
    at(11)
    for place, slot in ring:
        await_bytes(token_block(0, 0, half), tb_recv.at[slot, 1])
    if side == 4:
        for place, slot in ring:
            for batch, steps_in in enumerate(batches):
                await_bytes(
                    head_all.at[0 : len(steps_in) // 2 * rows, pair_lane(0)],
                    hr_recv.at[slot, batch],
                )
        for place, slot in ring:
            await_bytes(token_block(0, 0, half), tr_recv.at[slot])

    def make_logits(block, peak):
        part = jnp.dot(
            tokens[...].reshape(count, width),
            head_all[:, pair_lane(block)],
            preferred_element_type=F32,
        )
        logits[block] = part
        return jnp.maximum(peak, jnp.maximum(part[:, :LANES], part[:, LANES:]))

    peak = lax.fori_loop(0, side, make_logits, jnp.full((count, LANES), -jnp.inf, F32))
    peak = jnp.max(peak, axis=1, keepdims=True)
    total = jnp.zeros((count, LANES), F32)
    hit = jnp.zeros((count, LANES), F32)
    column = iota((count, LANES), 1).astype(F32)
    for block in range(side):
        for half in range(2):
            part = logits[block, :, half * LANES : (half + 1) * LANES]
            total = total + jnp.exp(part - peak)
            base = chip_at(block, b) * 2 * vocab_half + (z * 2 + half) * LANES
            hit = hit + jnp.where(wanted - base.astype(F32) == column, part, 0.0)
    total = jnp.sum(total, axis=1, keepdims=True)
    hit = jnp.sum(hit, axis=1, keepdims=True)
    column = iota((count, LANES), 1)
    packed = jnp.where(column == 0, peak, jnp.where(column == 1, total, hit))
    for step in range(per_set):
        turned = packed[step * LANES : (step + 1) * LANES].T
        local_stats[step] = turned[0:8]

    for step in range(per_set):
        to_z = rollouts[step]

        @pl.when(to_z == z)
        def _():
            column_stats[z] = local_stats[step]

        @pl.when(to_z != z)
        def _():
            remote(
                local_stats.at[step], column_stats.at[z], c0_send.at[step], c0_recv, to_z, chip, core
            ).start()

    def combine(parts):
        peaks = parts[:, 0:1, :]
        top = jnp.max(peaks, axis=0)
        sums = jnp.sum(parts[:, 1:2, :] * jnp.exp(peaks - top[None]), axis=0)
        return top, sums, jnp.sum(parts[:, 2:3, :], axis=0)

    mine = plane_stats.at[core, b]

    @pl.when(a == z_set)
    def _():
        await_bytes(column_stats.at[pl.ds(0, nz - 1)], c0_recv)
        plane_stats[core, b] = rows_of(*combine(column_stats[...]))

        def plane_start(step, carry):
            to_chip = wrap(chip + step, chips)
            remote(mine, mine, c1_send.at[0], c1_recv.at[core, b], z, to_chip, core).start()
            remote(mine, mine, c1_send.at[1], c1_recv.at[core, b], z, to_chip, other).start()
            return carry

        remote(mine, mine, c1_send.at[1], c1_recv.at[core, b], z, chip, other).start()
        lax.fori_loop(1, chips, plane_start, 0)

    for of_core in range(2):
        for at_b in range(side):
            theirs = plane_stats.at[of_core, at_b]
            ours = jnp.logical_and(
                jnp.logical_and(core == of_core, b == at_b), a == z_set
            )

            @pl.when(jnp.logical_not(ours))
            def _():
                await_bytes(theirs, c1_recv.at[of_core, at_b])

    logp = []
    for of_core in range(2):
        top, sums_all, hits = combine(plane_stats[of_core])
        logp.append(hits - top - jnp.log(sums_all))
    length = (count_ref[z] - 1) * 64 + last_ref[z]
    valid = iota((1, LANES), 1) < length
    row = jnp.where(valid, logp[0], 0.0)
    ratio = jnp.sum(jnp.where(valid, logp[0] - logp[1], 0.0), axis=1, keepdims=True)
    out_ref[...] = rows_of(row, jnp.broadcast_to(ratio, (1, LANES)))

    for copy in pair:
        copy.wait_send()
    for copy in moves + picks + line + cross + sums + crosses + list(sends.values()):
        copy.wait_send()
    await_bytes(targets_all.at[pl.ds(0, nz - 1)], tgt_send)
    await_bytes(stats.at[pl.ds(0, chips - 1)], stat_send)
    await_bytes(head_all.at[0 : (nz - 1) * rows, pair_lane(0)], hz_send)
    for place, slot in ring:
        await_bytes(head_all.at[:, pair_lane(0)], hf_send.at[slot])
        await_bytes(token_block(0, 0, side), tb_send.at[slot])
    sent = tokens.at[:, :, pl.ds(0, len(near) * LANES)]

    @pl.when(gap == 0)
    def _():
        await_bytes(sent, ta_send)

    @pl.when(gap != 0)
    def _():
        await_bytes(tokens.at[:, :, pl.ds(0, side * LANES)], ta_send)

    if side == 4:
        await_bytes(head_all.at[:, pair_lane(0)], hr_send)
        await_bytes(token_block(0, 0, side), tr_send)
    for step in range(per_set):

        @pl.when(rollouts[step] != z)
        def _():
            await_bytes(local_stats.at[step], c0_send.at[step])

    @pl.when(a == z_set)
    def _():
        await_bytes(stats.at[pl.ds(0, chips - 1)], c1_send.at[0])
        await_bytes(stats, c1_send.at[1])


def body(
    nz,
    side,
    pages,
    page_table,
    page_count,
    last_len,
    targets,
    mix_key,
    w_key,
    w_value,
    ln_gain,
    ln_bias,
    head,
):
    chips = side * side
    per_set = nz // side
    width = chips * LANES
    units = w_key.shape[2]
    rows = head.shape[1]
    vmem = pl.BlockSpec(memory_space=pltpu.VMEM)
    hbm = pl.BlockSpec(memory_space=pl.ANY)
    dma = pltpu.SemaphoreType.DMA
    batches = len(BATCHES[nz])
    share = LANES // (2 * chips)
    semaphores = [6, 6, 14, (), ()]
    semaphores += [4] * 2 + [per_set] * 2 + [side] * 8
    semaphores += [(), (), (), batches, 2, (2, batches), (), (2, batches)]
    semaphores += [per_set] * 2 + [(), side, 2, (2, 2), (), 2]
    semaphores += [per_set, (), 2, (2, side)]
    result = pl.pallas_call(
        functools.partial(kernel, nz, side),
        out_shape=jax.ShapeDtypeStruct((8, LANES), F32),
        in_specs=[hbm] * 11,
        out_specs=vmem,
        scratch_shapes=[
            pltpu.SMEM(page_table.shape[::-1], jnp.int32),
            pltpu.SMEM(page_count.shape, jnp.int32),
            pltpu.SMEM(last_len.shape, jnp.int32),
            pltpu.VMEM(pages.shape, BF16),
            pltpu.VMEM(mix_key.shape, F32),
            pltpu.VMEM(ln_gain.shape, F32),
            pltpu.VMEM(ln_bias.shape, F32),
            pltpu.VMEM(pages.shape[1:], BF16),
            pltpu.VMEM(mix_key.shape, F32),
            pltpu.VMEM((nz, 1, LANES), jnp.int32),
            pltpu.VMEM((2, rows, head.shape[2]), BF16),
            pltpu.VMEM((width, 2 * side * LANES), BF16),
            pltpu.VMEM((width, 2 * units), BF16),
            pltpu.VMEM((2 * units, width), BF16),
            pltpu.VMEM((side * 4, 64, LANES), BF16),
            pltpu.VMEM((per_set, 2, 64, LANES), BF16),
            pltpu.VMEM((per_set, 2, 64, LANES), BF16),
            pltpu.VMEM((side, side, LANES, LANES), BF16),
            pltpu.VMEM((LANES, width), BF16),
            pltpu.VMEM((LANES, 2 * units), BF16),
            pltpu.VMEM((side, side, LANES, LANES), F32),
            pltpu.VMEM((side, side, LANES, LANES), F32),
            pltpu.VMEM((side, LANES, LANES), F32),
            pltpu.VMEM((side, LANES, LANES), F32),
            pltpu.VMEM((chips, 8, LANES), F32),
            pltpu.VMEM((per_set, LANES, LANES), BF16),
            pltpu.VMEM((per_set, LANES, width), BF16),
            pltpu.VMEM((side, per_set * LANES, 2 * LANES), F32),
            pltpu.VMEM((per_set, 8, LANES), F32),
            pltpu.VMEM((nz, 8, LANES), F32),
            pltpu.VMEM((2, side, 8, LANES), F32),
        ]
        + [dma(size if isinstance(size, tuple) else (size,)) for size in semaphores],
        compiler_params=pltpu.CompilerParams(
            collective_id=0, has_side_effects=True, vmem_limit_bytes=VMEM_LIMIT
        ),
    )(
        page_table.T,
        page_count,
        last_len,
        pages,
        mix_key,
        targets,
        ln_gain,
        ln_bias,
        w_key,
        w_value,
        head,
    )
    start = lax.axis_index("tensor") * share
    return lax.dynamic_slice(result, (0, start), (1, share)), result[1, 0:1]


def solution(mesh):
    nz = mesh.shape["dp"]
    side = {32: 4, 8: 2}[mesh.shape["tensor"]]
    specs = (
        P(None, "dp", None, "tensor"),
        P(),
        P(),
        P(),
        P("dp", None),
        P(None, "tensor"),
        P(None, None, "tensor"),
        P(None, "tensor", None),
        P(),
        P(),
        P(None, "dp", "tensor"),
    )
    return jax.shard_map(
        functools.partial(body, nz, side),
        mesh=mesh,
        in_specs=specs,
        out_specs=(P("dp", "tensor"), P("dp")),
        check_vma=False,
    )
```

```python
import functools

import jax
import jax.numpy as jnp
from jax import lax
from jax.experimental import pallas as pl
from jax.experimental.pallas import tpu as pltpu
from jax.sharding import PartitionSpec as P

epsilon = 1e-05
F32 = jnp.float32
BF16 = jnp.bfloat16
LANES = 128
BATCHES = {16: ((0, 1, 15, 2), (14, 3, 13, 8), (4, 12, 7, 9), (5, 11, 6, 10)), 4: ((0, 2), (1, 3))}
VMEM_LIMIT = 63 * 1024 * 1024


ORDER = {4: (0, 1, 3, 2), 2: (0, 1)}
PARTS = {4: ((0, 3, (1, 3)), (3, 1, (2,))), 2: ((0, 1, ()), (1, 1, (1,)))}
SCHEDULE = {
    0: (("s", 0),),
    1: (("s", 1), ("s", 2)),
    2: (("s", 3),),
    4: (("f", 0),),
    5: (("f", 1), ("r", 0)),
    7: (("f", 2), ("r", 1)),
    9: (("f", 3), ("r", 2)),
    10: (("r", 3),),
}


def iota(shape, axis):
    return lax.broadcasted_iota(jnp.int32, shape, axis)


def rows_of(*rows):
    place = iota((8, LANES), 0)
    tile = jnp.zeros((8, LANES), F32)
    for index, row in enumerate(rows):
        tile = jnp.where(place == index, jnp.broadcast_to(row, (8, LANES)), tile)
    return tile


def column_of(row):
    return jnp.broadcast_to(row, (LANES, LANES)).T


def kernel(
    nz,
    side,
    table_hbm,
    count_hbm,
    last_hbm,
    pages_hbm,
    mix_hbm,
    target_hbm,
    gain_hbm,
    bias_hbm,
    wk_hbm,
    wv_hbm,
    head_hbm,
    out_ref,
    table_ref,
    count_ref,
    last_ref,
    pages_ref,
    mix_ref,
    gain_ref,
    bias_ref,
    pages_in,
    mix_in,
    targets_all,
    head_src,
    head_all,
    wk_all,
    wv_all,
    window,
    chosen,
    picked,
    shift_blocks,
    shifted_all,
    act,
    partial,
    line_sums,
    line_total,
    cross_sums,
    stats,
    sets,
    tokens,
    logits,
    local_stats,
    column_stats,
    plane_stats,
    pair_send,
    pair_recv,
    load_sem,
    tgt_send,
    tgt_recv,
    win_send,
    win_recv,
    pick_send,
    pick_recv,
    sa_send,
    sa_recv,
    sb_send,
    sb_recv,
    ra_send,
    ra_recv,
    rb_send,
    rb_recv,
    stat_send,
    stat_recv,
    hz_send,
    hz_recv,
    hf_send,
    hf_recv,
    hr_send,
    hr_recv,
    set_send,
    set_recv,
    ta_send,
    ta_recv,
    tb_send,
    tb_recv,
    tr_send,
    tr_recv,
    c0_send,
    c0_recv,
    c1_send,
    c1_recv,
):
    chips = side * side
    per_set = nz // side
    z = lax.axis_index("dp")
    tensor = lax.axis_index("tensor")
    core = lax.rem(tensor, 2)
    other = 1 - core
    chip = tensor // 2
    x = chip // side
    y = lax.rem(chip, side)
    a = x * other + y * core
    b = y * other + x * core
    z_set = lax.rem(z, side)
    sign = 1 - 2 * core
    width = chips * LANES
    units = wk_hbm.shape[2]
    vocab_half = head_hbm.shape[2]
    rows = head_hbm.shape[1]
    slots = nz // 2
    near = {4: (1, -1, 2), 2: (1,)}[side]
    steps = (1, 3, 2) if side == 4 else (1,)
    ring = ((1, 0), (side - 1, 1)) if side == 4 else ((1, 0),)
    batches = BATCHES[nz]
    count = per_set * LANES
    order = ORDER[per_set]
    parts = PARTS[per_set]

    def wrap(value, size):
        return lax.rem(value + 4 * size, size)

    gap = wrap(a - z_set, side)
    if side == 4:
        gap = gap - 4 * (gap // 3) + 2 * (sign - 1) * (gap // 2 - gap // 3)
    else:
        gap = gap * sign
    from_z = wrap(z + gap, nz)

    def chip_at(at_a, at_b):
        return (at_a * side + at_b) * other + (at_b * side + at_a) * core

    def remote(src, dst, send, recv, to_z, to_chip, to_core):
        return pltpu.make_async_remote_copy(
            src_ref=src,
            dst_ref=dst,
            send_sem=send,
            recv_sem=recv,
            device_id={"dp": to_z, "tensor": to_chip * 2 + to_core},
            device_id_type=pl.DeviceIdType.MESH,
        )

    def await_bytes(view, sem):
        pltpu.make_async_copy(view, view, sem).wait()

    def lane(index):
        return pl.ds(pl.multiple_of(index * LANES, LANES), LANES)

    def pair_lane(index):
        return pl.ds(pl.multiple_of(index * 2 * LANES, 2 * LANES), 2 * LANES)

    def in_line(step):
        return chip_at(wrap(a + step, side), b)

    def across(step):
        return chip_at(a, wrap(b + step, side))

    unit_cols = pl.ds(pl.multiple_of(core * units, units), units)
    loads = (
        pltpu.make_async_copy(wk_hbm.at[core], wk_all.at[:, unit_cols], load_sem.at[0]),
        pltpu.make_async_copy(wv_hbm.at[core], wv_all.at[unit_cols, :], load_sem.at[1]),
        pltpu.make_async_copy(head_hbm.at[core], head_src.at[core], load_sem.at[2]),
    )
    small = (
        pltpu.make_async_copy(pages_hbm, pages_ref, load_sem.at[6]),
        pltpu.make_async_copy(mix_hbm, mix_ref, load_sem.at[7]),
        pltpu.make_async_copy(target_hbm, targets_all.at[z], load_sem.at[8]),
        pltpu.make_async_copy(gain_hbm, gain_ref, load_sem.at[9]),
        pltpu.make_async_copy(bias_hbm, bias_ref, load_sem.at[10]),
        pltpu.make_async_copy(table_hbm, table_ref, load_sem.at[11]),
        pltpu.make_async_copy(count_hbm, count_ref, load_sem.at[12]),
        pltpu.make_async_copy(last_hbm, last_ref, load_sem.at[13]),
    )
    for load in small + loads:
        load.start()

    barrier = pltpu.get_barrier_semaphore()

    def hello(to_z, to_chip, to_core):
        pl.semaphore_signal(
            barrier,
            inc=1,
            device_id={"dp": to_z, "tensor": to_chip * 2 + to_core},
            device_id_type=pl.DeviceIdType.MESH,
        )

    hello(z, chip, other)

    def hello_z(step, carry):
        hello(wrap(z + step, nz), chip, core)
        return carry

    def hello_plane(step, carry):
        hello(z, wrap(chip + step, chips), core)
        hello(z, wrap(chip + step, chips), other)
        return carry

    @pl.when(gap != 0)
    def _():
        for at_a in range(side):
            hello(from_z, chip_at(at_a, b), core)

    lax.fori_loop(1, nz, hello_z, 0)
    lax.fori_loop(1, chips, hello_plane, 0)
    for load in small:
        load.wait()
    pl.semaphore_wait(barrier, nz - 1 + 2 * (chips - 1) + 1 + len(near))

    pair = (
        remote(pages_ref.at[other], pages_in, pair_send.at[0], pair_recv.at[0], z, chip, other),
        remote(mix_ref, mix_in, pair_send.at[1], pair_recv.at[1], z, chip, other),
        remote(
            head_hbm.at[other], head_src.at[core], pair_send.at[2], pair_recv.at[2], z, chip, other
        ),
        remote(
            wk_hbm.at[other],
            wk_all.at[:, unit_cols],
            pair_send.at[3],
            pair_recv.at[3],
            z,
            chip,
            other,
        ),
        remote(
            wv_hbm.at[other],
            wv_all.at[unit_cols, :],
            pair_send.at[4],
            pair_recv.at[4],
            z,
            chip,
            other,
        ),
    )
    for copy in pair:
        copy.start()

    def head_row(index):
        place = (lax.rem(index, side) * side + index // side) * other + index * core
        return pl.ds(pl.multiple_of(place * rows, rows), rows)

    def head_piece(to_z):
        return head_src.at[to_z // slots, :, pair_lane(lax.rem(to_z, slots))]

    keep = pltpu.make_async_copy(
        head_piece(z), head_all.at[head_row(z), pair_lane(a)], load_sem.at[3]
    )

    def head_start(batch):
        for step in batches[batch]:
            if step == 0:
                keep.start()
                continue
            remote(
                head_piece(wrap(z + step, nz)),
                head_all.at[head_row(z), pair_lane(a)],
                hz_send,
                hz_recv.at[batch],
                wrap(z + step, nz),
                chip,
                core,
            ).start()

    def head_forward(batch):
        steps_in = batches[batch]
        if 0 in steps_in:
            keep.wait()
        arrived = len(steps_in) - (0 in steps_in)
        await_bytes(head_all.at[0 : arrived * rows, pair_lane(a)], hz_recv.at[batch])
        for step in steps_in:
            block = head_all.at[head_row(wrap(z - step, nz)), pair_lane(a)]
            for place, slot in ring:
                remote(
                    block, block, hf_send.at[slot], hf_recv.at[slot, batch], z, in_line(place), core
                ).start()

    def head_relay(batch):
        steps_in = batches[batch]
        for place, slot in ring:
            await_bytes(
                head_all.at[0 : len(steps_in) * rows, pair_lane(0)], hf_recv.at[slot, batch]
            )
        if side < 4:
            return
        for index, step in enumerate(steps_in):
            place, slot = ring[index % 2]
            source = wrap(a - place, side)
            block = head_all.at[head_row(wrap(z - step, nz)), pair_lane(source)]
            remote(
                block, block, hr_send, hr_recv.at[slot, batch], z, in_line(place), core
            ).start()

    def at(point):
        for action, batch in SCHEDULE.get(point, ()):
            if batch >= len(batches):
                continue
            if (action, batch) == ("s", 0):
                loads[2].wait()
                pair[2].wait_recv()
            {"s": head_start, "f": head_forward, "r": head_relay}[action](batch)

    pair[0].wait_recv()
    ours = pages_ref[core]
    theirs = pages_in[...]

    @pl.when(core == 0)
    def _():
        window[pl.ds(4, 4)] = jnp.concatenate([ours, theirs], axis=-1)

    @pl.when(core == 1)
    def _():
        window[pl.ds(4, 4)] = jnp.concatenate([theirs, ours], axis=-1)

    window_offsets = {4: (-1, 0, 1, 2), 2: (-1, 0)}[side]
    mine = window.at[pl.ds(4, 4)]
    moves = []
    for slot, offset in enumerate(window_offsets):
        if offset == 0:
            continue
        copy = remote(
            mine,
            window.at[pl.ds(slot * 4, 4)],
            win_send.at[slot],
            win_recv.at[slot],
            wrap(z - sign * offset, nz),
            chip,
            core,
        )
        copy.start()
        moves.append(copy)

    at(0)
    for copy in moves:
        copy.wait_recv()

    picks = []
    for step in range(per_set):
        to_z = wrap(z + side * step, nz)
        for page in range(2):
            entry = table_ref[page, to_z]
            slot = lax.rem((entry // 4 - z) * sign + 1 + 4 * nz, nz)
            wanted = jnp.logical_and(slot < side, page < count_ref[to_z])
            flag = jnp.where(wanted, 1.0, 0.0).astype(F32)
            index = jnp.minimum(slot, side - 1) * 4 + lax.rem(entry, 4)
            block = (window[index].astype(F32) * flag).astype(BF16)
            if step == 0:
                picked[0, page] = block
            else:
                chosen[step, page] = block
        if step > 0:
            copy = remote(
                chosen.at[step],
                picked.at[step],
                pick_send.at[step],
                pick_recv.at[step],
                to_z,
                chip,
                core,
            )
            copy.start()
            picks.append(copy)

    at(1)

    def send_target(step, carry):
        remote(
            targets_all.at[z],
            targets_all.at[z],
            tgt_send,
            tgt_recv,
            wrap(z + step, nz),
            chip,
            core,
        ).start()
        return carry

    lax.fori_loop(1, nz, send_target, 0)

    pair[1].wait_recv()
    for copy in picks:
        copy.wait_recv()
    state = picked[0].astype(F32)
    for step in range(1, per_set):
        state = state + picked[step].astype(F32)
    state = state.reshape(LANES, LANES)
    rolled = pltpu.roll(state, 1, 0)
    previous = jnp.where(iota((LANES, LANES), 0) == 0, 0.0, rolled)
    model = core.astype(F32)

    def of_model(pair_rows):
        return pair_rows[0:1] * (1.0 - model) + pair_rows[1:2] * model

    ours = of_model(mix_ref[...])
    theirs = of_model(mix_in[...])
    low = jnp.concatenate([ours, theirs], axis=-1)
    high = jnp.concatenate([theirs, ours], axis=-1)
    mix = low * (1.0 - model) + high * model
    shift_blocks[b, a] = (state + (previous - state) * mix).astype(BF16)

    line = []
    for index, step in enumerate(steps):
        block = shift_blocks.at[b, a]
        copy = remote(block, block, sa_send.at[index], sa_recv.at[index], z, in_line(step), core)
        copy.start()
        line.append(copy)
    at(2)
    for copy in line:
        copy.wait_recv()
    cross = []
    for index, step in enumerate(steps):
        block = shift_blocks.at[b]
        copy = remote(block, block, sb_send.at[index], sb_recv.at[index], z, across(step), core)
        copy.start()
        cross.append(copy)
    at(3)
    loads[0].wait()
    loads[1].wait()
    pair[3].wait_recv()
    pair[4].wait_recv()
    for copy in cross:
        copy.wait_recv()
    for at_b in range(side):
        for at_a in range(side):
            shifted_all[:, lane(chip_at(at_a, at_b))] = shift_blocks[at_b, at_a]

    hidden = jnp.dot(shifted_all[...], wk_all[...], preferred_element_type=F32)
    act[...] = (jnp.maximum(hidden, 0.0) ** 2).astype(BF16)
    sums = []
    for index, step in enumerate((side // 2,) + tuple(s for s in steps if s != side // 2) + (0,)):
        to_a = wrap(a + step, side)

        def mix_out(to_b, carry):
            cols = lane(chip_at(to_a, to_b))
            partial[to_a, to_b] = jnp.dot(
                act[...], wv_all[:, cols], preferred_element_type=F32
            )
            return carry

        lax.fori_loop(0, side, mix_out, 0)
        if step:
            copy = remote(
                partial.at[to_a],
                line_sums.at[step],
                ra_send.at[step],
                ra_recv.at[step],
                z,
                in_line(step),
                core,
            )
            copy.start()
            sums.append(copy)
    at(4)
    total = partial[a]
    for copy in sums:
        copy.wait_recv()
    for step in steps:
        total = total + line_sums[step]
    line_total[...] = total
    crosses = []
    for step in steps:
        copy = remote(
            line_total.at[wrap(b + step, side)],
            cross_sums.at[step],
            rb_send.at[step],
            rb_recv.at[step],
            z,
            across(step),
            core,
        )
        copy.start()
        crosses.append(copy)
    at(5)
    residual = state + line_total[b]
    for step, copy in zip(steps, crosses):
        copy.wait_recv()
    for step in steps:
        residual = residual + cross_sums[step]

    turned = residual.T
    stats[chip] = rows_of(
        jnp.sum(turned, axis=0, keepdims=True), jnp.sum(turned * turned, axis=0, keepdims=True)
    )

    def stat_start(step, carry):
        remote(
            stats.at[chip],
            stats.at[chip],
            stat_send,
            stat_recv,
            z,
            wrap(chip + step, chips),
            core,
        ).start()
        return carry

    lax.fori_loop(1, chips, stat_start, 0)
    at(6)
    await_bytes(stats.at[pl.ds(0, chips - 1)], stat_recv)
    total = jnp.sum(stats[...], axis=0)
    average = total[0:1] / width
    variance = total[1:2] / width - average * average
    scale = lax.rsqrt(variance + epsilon)
    gain = of_model(gain_ref[:, lane(chip)])
    bias = of_model(bias_ref[:, lane(chip)])
    normed = (residual - column_of(average)) * column_of(scale) * gain + bias
    sets[0] = normed.astype(BF16)

    sends = {}
    for step in range(1, per_set):
        slot = order.index(per_set - step)
        sends[step] = remote(
            sets.at[0],
            sets.at[slot],
            set_send.at[step],
            set_recv.at[step],
            wrap(z + side * step, nz),
            chip,
            core,
        )
        sends[step].start()
    at(7)

    def token_cols(at_b, at_a):
        return lane(at_b * side + at_a)

    def token_copy(first, size, at_a, to_z):
        return remote(
            sets.at[pl.ds(first, size)],
            tokens.at[pl.ds(first, size), :, token_cols(b, at_a)],
            ta_send,
            ta_recv.at[at_a],
            to_z,
            chip_at(z_set, b),
            core,
        )

    for index, (first, size, needs) in enumerate(parts):
        for step in needs:
            sends[step].wait_recv()
        for offset in reversed((0,) + near):
            if offset:
                token_copy(first, size, a, wrap(z - sign * offset, nz)).start()
                continue

            @pl.when(gap == 0)
            def _():
                tokens[first : first + size, :, token_cols(b, a)] = sets[first : first + size]

            @pl.when(gap != 0)
            def _():
                token_copy(first, size, a, z).start()

        at(8 + index)

    await_bytes(targets_all.at[pl.ds(0, nz - 1)], tgt_recv)
    rollouts = [wrap(from_z + side * step, nz) for step in order]
    wanted = jnp.concatenate(
        [column_of(targets_all[rollout].astype(F32)) for rollout in rollouts], axis=0
    )

    half = side // 2

    def token_block(at_b, first, size):
        start = pl.multiple_of((at_b * side + first) * LANES, LANES)
        return tokens.at[:, :, pl.ds(start, size * LANES)]

    for at_a in range(side):

        @pl.when(jnp.logical_not(jnp.logical_and(gap == 0, a == at_a)))
        def _():
            await_bytes(tokens.at[:, :, pl.ds(0, LANES)], ta_recv.at[at_a])

    for turn in range(2):
        for place, slot in ring:
            part = (turn + slot) % 2
            block = token_block(b, part * half, half)
            remote(
                block, block, tb_send.at[slot], tb_recv.at[slot, turn], z, across(place), core
            ).start()
    at(10)
    if side == 4:
        for place, slot in ring:
            await_bytes(token_block(0, 0, half), tb_recv.at[slot, 0])
            block = token_block(wrap(b - place, side), slot * half, half)
            remote(block, block, tr_send, tr_recv.at[slot], z, across(place), core).start()
    else:
        await_bytes(token_block(0, 0, half), tb_recv.at[0, 0])
    at(11)
    for place, slot in ring:
        await_bytes(token_block(0, 0, half), tb_recv.at[slot, 1])
    if side == 4:
        for place, slot in ring:
            for batch, steps_in in enumerate(batches):
                await_bytes(
                    head_all.at[0 : len(steps_in) // 2 * rows, pair_lane(0)],
                    hr_recv.at[slot, batch],
                )
        for place, slot in ring:
            await_bytes(token_block(0, 0, half), tr_recv.at[slot])

    def make_logits(block, peak):
        part = jnp.dot(
            tokens[...].reshape(count, width),
            head_all[:, pair_lane(block)],
            preferred_element_type=F32,
        )
        logits[block] = part
        return jnp.maximum(peak, jnp.maximum(part[:, :LANES], part[:, LANES:]))

    peak = lax.fori_loop(0, side, make_logits, jnp.full((count, LANES), -jnp.inf, F32))
    peak = jnp.max(peak, axis=1, keepdims=True)
    total = jnp.zeros((count, LANES), F32)
    hit = jnp.zeros((count, LANES), F32)
    column = iota((count, LANES), 1).astype(F32)
    for block in range(side):
        for half in range(2):
            part = logits[block, :, half * LANES : (half + 1) * LANES]
            total = total + jnp.exp(part - peak)
            base = chip_at(block, b) * 2 * vocab_half + (z * 2 + half) * LANES
            hit = hit + jnp.where(wanted - base.astype(F32) == column, part, 0.0)
    total = jnp.sum(total, axis=1, keepdims=True)
    hit = jnp.sum(hit, axis=1, keepdims=True)
    column = iota((count, LANES), 1)
    packed = jnp.where(column == 0, peak, jnp.where(column == 1, total, hit))
    for step in range(per_set):
        turned = packed[step * LANES : (step + 1) * LANES].T
        local_stats[step] = turned[0:8]

    for step in range(per_set):
        to_z = rollouts[step]

        @pl.when(to_z == z)
        def _():
            column_stats[z] = local_stats[step]

        @pl.when(to_z != z)
        def _():
            remote(
                local_stats.at[step], column_stats.at[z], c0_send.at[step], c0_recv, to_z, chip, core
            ).start()

    for copy in pair:
        copy.wait_send()
    for copy in moves + picks + line + cross + sums + crosses + list(sends.values()):
        copy.wait_send()
    await_bytes(targets_all.at[pl.ds(0, nz - 1)], tgt_send)
    await_bytes(stats.at[pl.ds(0, chips - 1)], stat_send)
    await_bytes(head_all.at[0 : (nz - 1) * rows, pair_lane(0)], hz_send)
    for place, slot in ring:
        await_bytes(head_all.at[:, pair_lane(0)], hf_send.at[slot])
        await_bytes(token_block(0, 0, side), tb_send.at[slot])
    sent = tokens.at[:, :, pl.ds(0, len(near) * LANES)]

    @pl.when(gap == 0)
    def _():
        await_bytes(sent, ta_send)

    @pl.when(gap != 0)
    def _():
        await_bytes(tokens.at[:, :, pl.ds(0, side * LANES)], ta_send)

    if side == 4:
        await_bytes(head_all.at[:, pair_lane(0)], hr_send)
        await_bytes(token_block(0, 0, side), tr_send)
    def combine(parts):
        peaks = parts[:, 0:1, :]
        top = jnp.max(peaks, axis=0)
        sums = jnp.sum(parts[:, 1:2, :] * jnp.exp(peaks - top[None]), axis=0)
        return top, sums, jnp.sum(parts[:, 2:3, :], axis=0)

    mine = plane_stats.at[core, b]

    @pl.when(a == z_set)
    def _():
        await_bytes(column_stats.at[pl.ds(0, nz - 1)], c0_recv)
        plane_stats[core, b] = rows_of(*combine(column_stats[...]))

        def plane_start(step, carry):
            to_chip = wrap(chip + step, chips)
            remote(mine, mine, c1_send.at[0], c1_recv.at[core, b], z, to_chip, core).start()
            remote(mine, mine, c1_send.at[1], c1_recv.at[core, b], z, to_chip, other).start()
            return carry

        remote(mine, mine, c1_send.at[1], c1_recv.at[core, b], z, chip, other).start()
        lax.fori_loop(1, chips, plane_start, 0)

    for of_core in range(2):
        for at_b in range(side):
            theirs = plane_stats.at[of_core, at_b]
            ours = jnp.logical_and(
                jnp.logical_and(core == of_core, b == at_b), a == z_set
            )

            @pl.when(jnp.logical_not(ours))
            def _():
                await_bytes(theirs, c1_recv.at[of_core, at_b])

    logp = []
    for of_core in range(2):
        top, sums_all, hits = combine(plane_stats[of_core])
        logp.append(hits - top - jnp.log(sums_all))
    length = (count_ref[z] - 1) * 64 + last_ref[z]
    valid = iota((1, LANES), 1) < length
    row = jnp.where(valid, logp[0], 0.0)
    ratio = jnp.sum(jnp.where(valid, logp[0] - logp[1], 0.0), axis=1, keepdims=True)
    out_ref[...] = rows_of(row, jnp.broadcast_to(ratio, (1, LANES)))

    for step in range(per_set):

        @pl.when(rollouts[step] != z)
        def _():
            await_bytes(local_stats.at[step], c0_send.at[step])

    @pl.when(a == z_set)
    def _():
        await_bytes(stats.at[pl.ds(0, chips - 1)], c1_send.at[0])
        await_bytes(stats, c1_send.at[1])


def body(
    nz,
    side,
    pages,
    page_table,
    page_count,
    last_len,
    targets,
    mix_key,
    w_key,
    w_value,
    ln_gain,
    ln_bias,
    head,
):
    chips = side * side
    per_set = nz // side
    width = chips * LANES
    units = w_key.shape[2]
    rows = head.shape[1]
    vmem = pl.BlockSpec(memory_space=pltpu.VMEM)
    hbm = pl.BlockSpec(memory_space=pl.ANY)
    dma = pltpu.SemaphoreType.DMA
    batches = len(BATCHES[nz])
    share = LANES // (2 * chips)
    semaphores = [6, 6, 14, (), ()]
    semaphores += [4] * 2 + [per_set] * 2 + [side] * 8
    semaphores += [(), (), (), batches, 2, (2, batches), (), (2, batches)]
    semaphores += [per_set] * 2 + [(), side, 2, (2, 2), (), 2]
    semaphores += [per_set, (), 2, (2, side)]
    result = pl.pallas_call(
        functools.partial(kernel, nz, side),
        out_shape=jax.ShapeDtypeStruct((8, LANES), F32),
        in_specs=[hbm] * 11,
        out_specs=vmem,
        scratch_shapes=[
            pltpu.SMEM(page_table.shape[::-1], jnp.int32),
            pltpu.SMEM(page_count.shape, jnp.int32),
            pltpu.SMEM(last_len.shape, jnp.int32),
            pltpu.VMEM(pages.shape, BF16),
            pltpu.VMEM(mix_key.shape, F32),
            pltpu.VMEM(ln_gain.shape, F32),
            pltpu.VMEM(ln_bias.shape, F32),
            pltpu.VMEM(pages.shape[1:], BF16),
            pltpu.VMEM(mix_key.shape, F32),
            pltpu.VMEM((nz, 1, LANES), jnp.int32),
            pltpu.VMEM((2, rows, head.shape[2]), BF16),
            pltpu.VMEM((width, 2 * side * LANES), BF16),
            pltpu.VMEM((width, 2 * units), BF16),
            pltpu.VMEM((2 * units, width), BF16),
            pltpu.VMEM((side * 4, 64, LANES), BF16),
            pltpu.VMEM((per_set, 2, 64, LANES), BF16),
            pltpu.VMEM((per_set, 2, 64, LANES), BF16),
            pltpu.VMEM((side, side, LANES, LANES), BF16),
            pltpu.VMEM((LANES, width), BF16),
            pltpu.VMEM((LANES, 2 * units), BF16),
            pltpu.VMEM((side, side, LANES, LANES), F32),
            pltpu.VMEM((side, side, LANES, LANES), F32),
            pltpu.VMEM((side, LANES, LANES), F32),
            pltpu.VMEM((side, LANES, LANES), F32),
            pltpu.VMEM((chips, 8, LANES), F32),
            pltpu.VMEM((per_set, LANES, LANES), BF16),
            pltpu.VMEM((per_set, LANES, width), BF16),
            pltpu.VMEM((side, per_set * LANES, 2 * LANES), F32),
            pltpu.VMEM((per_set, 8, LANES), F32),
            pltpu.VMEM((nz, 8, LANES), F32),
            pltpu.VMEM((2, side, 8, LANES), F32),
        ]
        + [dma(size if isinstance(size, tuple) else (size,)) for size in semaphores],
        compiler_params=pltpu.CompilerParams(
            collective_id=0, has_side_effects=True, vmem_limit_bytes=VMEM_LIMIT
        ),
    )(
        page_table.T,
        page_count,
        last_len,
        pages,
        mix_key,
        targets,
        ln_gain,
        ln_bias,
        w_key,
        w_value,
        head,
    )
    start = lax.axis_index("tensor") * share
    return lax.dynamic_slice(result, (0, start), (1, share)), result[1, 0:1]


def solution(mesh):
    nz = mesh.shape["dp"]
    side = {32: 4, 8: 2}[mesh.shape["tensor"]]
    specs = (
        P(None, "dp", None, "tensor"),
        P(),
        P(),
        P(),
        P("dp", None),
        P(None, "tensor"),
        P(None, None, "tensor"),
        P(None, "tensor", None),
        P(),
        P(),
        P(None, "dp", "tensor"),
    )
    return jax.shard_map(
        functools.partial(body, nz, side),
        mesh=mesh,
        in_specs=specs,
        out_specs=(P("dp", "tensor"), P("dp")),
        check_vma=False,
    )
```

```python
import functools

import jax
import jax.numpy as jnp
from jax import lax
from jax.experimental import pallas as pl
from jax.experimental.pallas import tpu as pltpu
from jax.sharding import PartitionSpec as P

epsilon = 1e-05
F32 = jnp.float32
BF16 = jnp.bfloat16
LANES = 128
BATCHES = {16: ((0, 1, 15, 2), (14, 3, 13, 8), (4, 12, 7, 9), (5, 11, 6, 10)), 4: ((0, 2), (1, 3))}
VMEM_LIMIT = 63 * 1024 * 1024


ORDER = {4: (0, 1, 3, 2), 2: (0, 1)}
PARTS = {4: ((0, 3, (1, 3)), (3, 1, (2,))), 2: ((0, 1, ()), (1, 1, (1,)))}
SCHEDULE = {
    0: (("s", 0),),
    1: (("s", 1), ("s", 2)),
    2: (("s", 3),),
    4: (("f", 0),),
    5: (("f", 1), ("r", 0)),
    7: (("f", 2), ("r", 1)),
    9: (("f", 3), ("r", 2)),
    10: (("r", 3),),
}


def iota(shape, axis):
    return lax.broadcasted_iota(jnp.int32, shape, axis)


def rows_of(*rows):
    place = iota((8, LANES), 0)
    tile = jnp.zeros((8, LANES), F32)
    for index, row in enumerate(rows):
        tile = jnp.where(place == index, jnp.broadcast_to(row, (8, LANES)), tile)
    return tile


def column_of(row):
    return jnp.broadcast_to(row, (LANES, LANES)).T


def kernel(
    nz,
    side,
    table_hbm,
    count_hbm,
    last_hbm,
    pages_hbm,
    mix_hbm,
    target_hbm,
    gain_hbm,
    bias_hbm,
    wk_hbm,
    wv_hbm,
    head_hbm,
    out_ref,
    table_ref,
    count_ref,
    last_ref,
    pages_ref,
    mix_ref,
    gain_ref,
    bias_ref,
    pages_in,
    mix_in,
    targets_all,
    head_src,
    head_all,
    wk_all,
    wv_all,
    window,
    chosen,
    picked,
    shift_blocks,
    shifted_all,
    act,
    partial,
    line_sums,
    line_total,
    cross_sums,
    stats,
    sets,
    tokens,
    logits,
    local_stats,
    column_stats,
    plane_stats,
    pair_send,
    pair_recv,
    load_sem,
    tgt_send,
    tgt_recv,
    win_send,
    win_recv,
    pick_send,
    pick_recv,
    sa_send,
    sa_recv,
    sb_send,
    sb_recv,
    ra_send,
    ra_recv,
    rb_send,
    rb_recv,
    stat_send,
    stat_recv,
    hz_send,
    hz_recv,
    hf_send,
    hf_recv,
    hr_send,
    hr_recv,
    set_send,
    set_recv,
    ta_send,
    ta_recv,
    tb_send,
    tb_recv,
    tr_send,
    tr_recv,
    c0_send,
    c0_recv,
    c1_send,
    c1_recv,
):
    chips = side * side
    per_set = nz // side
    z = lax.axis_index("dp")
    tensor = lax.axis_index("tensor")
    core = lax.rem(tensor, 2)
    other = 1 - core
    chip = tensor // 2
    x = chip // side
    y = lax.rem(chip, side)
    a = x * other + y * core
    b = y * other + x * core
    z_set = lax.rem(z, side)
    sign = 1 - 2 * core
    width = chips * LANES
    units = wk_hbm.shape[2]
    vocab_half = head_hbm.shape[2]
    rows = head_hbm.shape[1]
    slots = nz // 2
    near = {4: (1, -1, 2), 2: (1,)}[side]
    steps = (1, 3, 2) if side == 4 else (1,)
    ring = ((1, 0), (side - 1, 1)) if side == 4 else ((1, 0),)
    batches = BATCHES[nz]
    count = per_set * LANES
    order = ORDER[per_set]
    parts = PARTS[per_set]

    def wrap(value, size):
        return lax.rem(value + 4 * size, size)

    gap = wrap(a - z_set, side)
    if side == 4:
        gap = gap - 4 * (gap // 3) + 2 * (sign - 1) * (gap // 2 - gap // 3)
    else:
        gap = gap * sign
    from_z = wrap(z + gap, nz)

    def chip_at(at_a, at_b):
        return (at_a * side + at_b) * other + (at_b * side + at_a) * core

    def remote(src, dst, send, recv, to_z, to_chip, to_core):
        return pltpu.make_async_remote_copy(
            src_ref=src,
            dst_ref=dst,
            send_sem=send,
            recv_sem=recv,
            device_id={"dp": to_z, "tensor": to_chip * 2 + to_core},
            device_id_type=pl.DeviceIdType.MESH,
        )

    def await_bytes(view, sem):
        pltpu.make_async_copy(view, view, sem).wait()

    def lane(index):
        return pl.ds(pl.multiple_of(index * LANES, LANES), LANES)

    def pair_lane(index):
        return pl.ds(pl.multiple_of(index * 2 * LANES, 2 * LANES), 2 * LANES)

    def in_line(step):
        return chip_at(wrap(a + step, side), b)

    def across(step):
        return chip_at(a, wrap(b + step, side))

    unit_cols = pl.ds(pl.multiple_of(core * units, units), units)
    loads = (
        pltpu.make_async_copy(wk_hbm.at[core], wk_all.at[:, unit_cols], load_sem.at[0]),
        pltpu.make_async_copy(wv_hbm.at[core], wv_all.at[unit_cols, :], load_sem.at[1]),
        pltpu.make_async_copy(head_hbm.at[core], head_src.at[core], load_sem.at[2]),
    )
    small = (
        pltpu.make_async_copy(pages_hbm, pages_ref, load_sem.at[6]),
        pltpu.make_async_copy(mix_hbm, mix_ref, load_sem.at[7]),
        pltpu.make_async_copy(target_hbm, targets_all.at[z], load_sem.at[8]),
        pltpu.make_async_copy(gain_hbm, gain_ref, load_sem.at[9]),
        pltpu.make_async_copy(bias_hbm, bias_ref, load_sem.at[10]),
        pltpu.make_async_copy(table_hbm, table_ref, load_sem.at[11]),
        pltpu.make_async_copy(count_hbm, count_ref, load_sem.at[12]),
        pltpu.make_async_copy(last_hbm, last_ref, load_sem.at[13]),
    )
    for load in small + loads:
        load.start()

    barrier = pltpu.get_barrier_semaphore()

    def hello(to_z, to_chip, to_core):
        pl.semaphore_signal(
            barrier,
            inc=1,
            device_id={"dp": to_z, "tensor": to_chip * 2 + to_core},
            device_id_type=pl.DeviceIdType.MESH,
        )

    hello(z, chip, other)

    def hello_z(step, carry):
        hello(wrap(z + step, nz), chip, core)
        return carry

    def hello_plane(step, carry):
        hello(z, wrap(chip + step, chips), core)
        hello(z, wrap(chip + step, chips), other)
        return carry

    @pl.when(gap != 0)
    def _():
        for at_a in range(side):
            hello(from_z, chip_at(at_a, b), core)

    lax.fori_loop(1, nz, hello_z, 0)
    lax.fori_loop(1, chips, hello_plane, 0)
    for load in small:
        load.wait()
    pl.semaphore_wait(barrier, nz - 1 + 2 * (chips - 1) + 1 + len(near))

    pair = (
        remote(pages_ref.at[other], pages_in, pair_send.at[0], pair_recv.at[0], z, chip, other),
        remote(mix_ref, mix_in, pair_send.at[1], pair_recv.at[1], z, chip, other),
        remote(
            head_hbm.at[other], head_src.at[core], pair_send.at[2], pair_recv.at[2], z, chip, other
        ),
        remote(
            wk_hbm.at[other],
            wk_all.at[:, unit_cols],
            pair_send.at[3],
            pair_recv.at[3],
            z,
            chip,
            other,
        ),
        remote(
            wv_hbm.at[other],
            wv_all.at[unit_cols, :],
            pair_send.at[4],
            pair_recv.at[4],
            z,
            chip,
            other,
        ),
    )
    for copy in pair:
        copy.start()

    def head_row(index):
        place = (lax.rem(index, side) * side + index // side) * other + index * core
        return pl.ds(pl.multiple_of(place * rows, rows), rows)

    def head_piece(to_z):
        return head_src.at[to_z // slots, :, pair_lane(lax.rem(to_z, slots))]

    keep = pltpu.make_async_copy(
        head_piece(z), head_all.at[head_row(z), pair_lane(a)], load_sem.at[3]
    )

    def head_start(batch):
        for step in batches[batch]:
            if step == 0:
                keep.start()
                continue
            remote(
                head_piece(wrap(z + step, nz)),
                head_all.at[head_row(z), pair_lane(a)],
                hz_send,
                hz_recv.at[batch],
                wrap(z + step, nz),
                chip,
                core,
            ).start()

    def head_forward(batch):
        steps_in = batches[batch]
        if 0 in steps_in:
            keep.wait()
        arrived = len(steps_in) - (0 in steps_in)
        await_bytes(head_all.at[0 : arrived * rows, pair_lane(a)], hz_recv.at[batch])
        for step in steps_in:
            block = head_all.at[head_row(wrap(z - step, nz)), pair_lane(a)]
            for place, slot in ring:
                remote(
                    block, block, hf_send.at[slot], hf_recv.at[slot, batch], z, in_line(place), core
                ).start()

    def head_relay(batch):
        steps_in = batches[batch]
        for place, slot in ring:
            await_bytes(
                head_all.at[0 : len(steps_in) * rows, pair_lane(0)], hf_recv.at[slot, batch]
            )
        if side < 4:
            return
        for index, step in enumerate(steps_in):
            place, slot = ring[index % 2]
            source = wrap(a - place, side)
            block = head_all.at[head_row(wrap(z - step, nz)), pair_lane(source)]
            remote(
                block, block, hr_send, hr_recv.at[slot, batch], z, in_line(place), core
            ).start()

    def at(point):
        for action, batch in SCHEDULE.get(point, ()):
            if batch >= len(batches):
                continue
            if (action, batch) == ("s", 0):
                loads[2].wait()
                pair[2].wait_recv()
            {"s": head_start, "f": head_forward, "r": head_relay}[action](batch)

    pair[0].wait_recv()
    ours = pages_ref[core]
    theirs = pages_in[...]

    @pl.when(core == 0)
    def _():
        window[pl.ds(4, 4)] = jnp.concatenate([ours, theirs], axis=-1)

    @pl.when(core == 1)
    def _():
        window[pl.ds(4, 4)] = jnp.concatenate([theirs, ours], axis=-1)

    window_offsets = {4: (-1, 0, 1, 2), 2: (-1, 0)}[side]
    mine = window.at[pl.ds(4, 4)]
    moves = []
    for slot, offset in enumerate(window_offsets):
        if offset == 0:
            continue
        copy = remote(
            mine,
            window.at[pl.ds(slot * 4, 4)],
            win_send.at[slot],
            win_recv.at[slot],
            wrap(z - sign * offset, nz),
            chip,
            core,
        )
        copy.start()
        moves.append(copy)

    at(0)
    for copy in moves:
        copy.wait_recv()

    picks = []
    for step in range(per_set):
        to_z = wrap(z + side * step, nz)
        for page in range(2):
            entry = table_ref[page, to_z]
            slot = lax.rem((entry // 4 - z) * sign + 1 + 4 * nz, nz)
            wanted = jnp.logical_and(slot < side, page < count_ref[to_z])
            flag = jnp.where(wanted, 1.0, 0.0).astype(F32)
            index = jnp.minimum(slot, side - 1) * 4 + lax.rem(entry, 4)
            block = (window[index].astype(F32) * flag).astype(BF16)
            if step == 0:
                picked[0, page] = block
            else:
                chosen[step, page] = block
        if step > 0:
            copy = remote(
                chosen.at[step],
                picked.at[step],
                pick_send.at[step],
                pick_recv.at[step],
                to_z,
                chip,
                core,
            )
            copy.start()
            picks.append(copy)

    at(1)

    def send_target(step, carry):
        remote(
            targets_all.at[z],
            targets_all.at[z],
            tgt_send,
            tgt_recv,
            wrap(z + step, nz),
            chip,
            core,
        ).start()
        return carry

    lax.fori_loop(1, nz, send_target, 0)

    pair[1].wait_recv()
    for copy in picks:
        copy.wait_recv()
    state = picked[0].astype(F32)
    for step in range(1, per_set):
        state = state + picked[step].astype(F32)
    state = state.reshape(LANES, LANES)
    rolled = pltpu.roll(state, 1, 0)
    previous = jnp.where(iota((LANES, LANES), 0) == 0, 0.0, rolled)
    model = core.astype(F32)

    def of_model(pair_rows):
        return pair_rows[0:1] * (1.0 - model) + pair_rows[1:2] * model

    ours = of_model(mix_ref[...])
    theirs = of_model(mix_in[...])
    low = jnp.concatenate([ours, theirs], axis=-1)
    high = jnp.concatenate([theirs, ours], axis=-1)
    mix = low * (1.0 - model) + high * model
    shift_blocks[b, a] = (state + (previous - state) * mix).astype(BF16)

    line = []
    for index, step in enumerate(steps):
        block = shift_blocks.at[b, a]
        copy = remote(block, block, sa_send.at[index], sa_recv.at[index], z, in_line(step), core)
        copy.start()
        line.append(copy)
    at(2)
    for copy in line:
        copy.wait_recv()
    cross = []
    for index, step in enumerate(steps):
        block = shift_blocks.at[b]
        copy = remote(block, block, sb_send.at[index], sb_recv.at[index], z, across(step), core)
        copy.start()
        cross.append(copy)
    at(3)
    loads[0].wait()
    loads[1].wait()
    pair[3].wait_recv()
    pair[4].wait_recv()
    for copy in cross:
        copy.wait_recv()
    for at_b in range(side):
        for at_a in range(side):
            shifted_all[:, lane(chip_at(at_a, at_b))] = shift_blocks[at_b, at_a]

    hidden = jnp.dot(shifted_all[...], wk_all[...], preferred_element_type=F32)
    act[...] = (jnp.maximum(hidden, 0.0) ** 2).astype(BF16)
    sums = []
    for index, step in enumerate((side // 2,) + tuple(s for s in steps if s != side // 2) + (0,)):
        to_a = wrap(a + step, side)

        def mix_out(to_b, carry):
            cols = lane(chip_at(to_a, to_b))
            partial[to_a, to_b] = jnp.dot(
                act[...], wv_all[:, cols], preferred_element_type=F32
            )
            return carry

        lax.fori_loop(0, side, mix_out, 0)
        if step:
            copy = remote(
                partial.at[to_a],
                line_sums.at[step],
                ra_send.at[step],
                ra_recv.at[step],
                z,
                in_line(step),
                core,
            )
            copy.start()
            sums.append(copy)
    at(4)
    total = partial[a]
    for copy in sums:
        copy.wait_recv()
    for step in steps:
        total = total + line_sums[step]
    line_total[...] = total
    crosses = []
    for step in steps:
        copy = remote(
            line_total.at[wrap(b + step, side)],
            cross_sums.at[step],
            rb_send.at[step],
            rb_recv.at[step],
            z,
            across(step),
            core,
        )
        copy.start()
        crosses.append(copy)
    at(5)
    residual = state + line_total[b]
    for step, copy in zip(steps, crosses):
        copy.wait_recv()
    for step in steps:
        residual = residual + cross_sums[step]

    turned = residual.T
    stats[chip] = rows_of(
        jnp.sum(turned, axis=0, keepdims=True), jnp.sum(turned * turned, axis=0, keepdims=True)
    )

    def stat_start(step, carry):
        remote(
            stats.at[chip],
            stats.at[chip],
            stat_send,
            stat_recv,
            z,
            wrap(chip + step, chips),
            core,
        ).start()
        return carry

    lax.fori_loop(1, chips, stat_start, 0)
    at(6)
    await_bytes(stats.at[pl.ds(0, chips - 1)], stat_recv)
    total = jnp.sum(stats[...], axis=0)
    average = total[0:1] / width
    variance = total[1:2] / width - average * average
    scale = lax.rsqrt(variance + epsilon)
    gain = of_model(gain_ref[:, lane(chip)])
    bias = of_model(bias_ref[:, lane(chip)])
    normed = (residual - column_of(average)) * column_of(scale) * gain + bias
    sets[0] = normed.astype(BF16)

    sends = {}
    for step in range(1, per_set):
        slot = order.index(per_set - step)
        sends[step] = remote(
            sets.at[0],
            sets.at[slot],
            set_send.at[step],
            set_recv.at[step],
            wrap(z + side * step, nz),
            chip,
            core,
        )
        sends[step].start()
    at(7)

    def token_cols(at_b, at_a):
        return lane(at_b * side + at_a)

    def token_copy(index, first, size, at_a, to_z):
        return remote(
            sets.at[pl.ds(first, size)],
            tokens.at[pl.ds(first, size), :, token_cols(b, at_a)],
            ta_send,
            ta_recv.at[index, at_a],
            to_z,
            chip_at(z_set, b),
            core,
        )

    for index, (first, size, needs) in enumerate(parts):
        for step in needs:
            sends[step].wait_recv()
        for offset in reversed((0,) + near):
            if offset:
                token_copy(index, first, size, a, wrap(z - sign * offset, nz)).start()
                continue

            @pl.when(gap == 0)
            def _():
                tokens[first : first + size, :, token_cols(b, a)] = sets[first : first + size]

            @pl.when(gap != 0)
            def _():
                token_copy(index, first, size, a, z).start()

        at(8 + index)

    await_bytes(targets_all.at[pl.ds(0, nz - 1)], tgt_recv)
    rollouts = [wrap(from_z + side * step, nz) for step in order]
    wanted = jnp.concatenate(
        [column_of(targets_all[rollout].astype(F32)) for rollout in rollouts], axis=0
    )

    half = side // 2

    def token_block(index, at_b, first, size):
        start = pl.multiple_of((at_b * side + first) * LANES, LANES)
        low, height, _ = parts[index]
        return tokens.at[pl.ds(low, height), :, pl.ds(start, size * LANES)]

    for index, (first, size, _) in enumerate(parts):
        for at_a in range(side):

            @pl.when(jnp.logical_not(jnp.logical_and(gap == 0, a == at_a)))
            def _():
                await_bytes(token_block(index, 0, 0, 1), ta_recv.at[index, at_a])

        for turn in range(2):
            for place, slot in ring:
                block = token_block(index, b, (turn + slot) % 2 * half, half)
                remote(
                    block,
                    block,
                    tb_send.at[slot, index],
                    tb_recv.at[slot, index, turn],
                    z,
                    across(place),
                    core,
                ).start()
    at(10)
    for index in range(len(parts)):
        for place, slot in ring:
            await_bytes(token_block(index, 0, 0, half), tb_recv.at[slot, index, 0])
            if side == 4:
                block = token_block(index, wrap(b - place, side), slot * half, half)
                remote(
                    block,
                    block,
                    tr_send.at[index],
                    tr_recv.at[slot, index],
                    z,
                    across(place),
                    core,
                ).start()
    at(11)
    if side == 4:
        for place, slot in ring:
            for batch, steps_in in enumerate(batches):
                await_bytes(
                    head_all.at[0 : len(steps_in) // 2 * rows, pair_lane(0)],
                    hr_recv.at[slot, batch],
                )

    depth = side * LANES

    def add_logits(place, first):
        cols = pl.ds(pl.multiple_of(wrap(b + place, side) * depth, depth), depth)

        def block_step(block, carry):
            part = jnp.dot(
                tokens[:, :, cols].reshape(count, depth),
                head_all[cols, pair_lane(block)],
                preferred_element_type=F32,
            )
            logits[block] = part if first else logits[block] + part
            return carry

        lax.fori_loop(0, side, block_step, 0)

    add_logits(0, True)
    for place, slot in ring:
        for index in range(len(parts)):
            await_bytes(token_block(index, 0, 0, half), tb_recv.at[slot, index, 1])
        add_logits(-place, False)
    if side == 4:
        for place, slot in ring:
            for index in range(len(parts)):
                await_bytes(token_block(index, 0, 0, half), tr_recv.at[slot, index])
        add_logits(2, False)
    peak = jnp.full((count, LANES), -jnp.inf, F32)
    for block in range(side):
        part = logits[block]
        peak = jnp.maximum(peak, jnp.maximum(part[:, :LANES], part[:, LANES:]))
    peak = jnp.max(peak, axis=1, keepdims=True)
    total = jnp.zeros((count, LANES), F32)
    hit = jnp.zeros((count, LANES), F32)
    column = iota((count, LANES), 1).astype(F32)
    for block in range(side):
        for half in range(2):
            part = logits[block, :, half * LANES : (half + 1) * LANES]
            total = total + jnp.exp(part - peak)
            base = chip_at(block, b) * 2 * vocab_half + (z * 2 + half) * LANES
            hit = hit + jnp.where(wanted - base.astype(F32) == column, part, 0.0)
    total = jnp.sum(total, axis=1, keepdims=True)
    hit = jnp.sum(hit, axis=1, keepdims=True)
    column = iota((count, LANES), 1)
    packed = jnp.where(column == 0, peak, jnp.where(column == 1, total, hit))
    for step in range(per_set):
        turned = packed[step * LANES : (step + 1) * LANES].T
        local_stats[step] = turned[0:8]

    for step in range(per_set):
        to_z = rollouts[step]

        @pl.when(to_z == z)
        def _():
            column_stats[z] = local_stats[step]

        @pl.when(to_z != z)
        def _():
            remote(
                local_stats.at[step], column_stats.at[z], c0_send.at[step], c0_recv, to_z, chip, core
            ).start()

    for copy in pair:
        copy.wait_send()
    for copy in moves + picks + line + cross + sums + crosses + list(sends.values()):
        copy.wait_send()
    await_bytes(targets_all.at[pl.ds(0, nz - 1)], tgt_send)
    await_bytes(stats.at[pl.ds(0, chips - 1)], stat_send)
    await_bytes(head_all.at[0 : (nz - 1) * rows, pair_lane(0)], hz_send)
    for place, slot in ring:
        await_bytes(head_all.at[:, pair_lane(0)], hf_send.at[slot])
        for index in range(len(parts)):
            await_bytes(token_block(index, 0, 0, side), tb_send.at[slot, index])
    sent = tokens.at[:, :, pl.ds(0, len(near) * LANES)]

    @pl.when(gap == 0)
    def _():
        await_bytes(sent, ta_send)

    @pl.when(gap != 0)
    def _():
        await_bytes(tokens.at[:, :, pl.ds(0, side * LANES)], ta_send)

    if side == 4:
        await_bytes(head_all.at[:, pair_lane(0)], hr_send)
        for index in range(len(parts)):
            await_bytes(token_block(index, 0, 0, side), tr_send.at[index])
    def combine(parts):
        peaks = parts[:, 0:1, :]
        top = jnp.max(peaks, axis=0)
        sums = jnp.sum(parts[:, 1:2, :] * jnp.exp(peaks - top[None]), axis=0)
        return top, sums, jnp.sum(parts[:, 2:3, :], axis=0)

    mine = plane_stats.at[core, b]

    @pl.when(a == z_set)
    def _():
        await_bytes(column_stats.at[pl.ds(0, nz - 1)], c0_recv)
        plane_stats[core, b] = rows_of(*combine(column_stats[...]))

        def plane_start(step, carry):
            to_chip = wrap(chip + step, chips)
            remote(mine, mine, c1_send.at[0], c1_recv.at[core, b], z, to_chip, core).start()
            remote(mine, mine, c1_send.at[1], c1_recv.at[core, b], z, to_chip, other).start()
            return carry

        remote(mine, mine, c1_send.at[1], c1_recv.at[core, b], z, chip, other).start()
        lax.fori_loop(1, chips, plane_start, 0)

    for of_core in range(2):
        for at_b in range(side):
            theirs = plane_stats.at[of_core, at_b]
            ours = jnp.logical_and(
                jnp.logical_and(core == of_core, b == at_b), a == z_set
            )

            @pl.when(jnp.logical_not(ours))
            def _():
                await_bytes(theirs, c1_recv.at[of_core, at_b])

    logp = []
    for of_core in range(2):
        top, sums_all, hits = combine(plane_stats[of_core])
        logp.append(hits - top - jnp.log(sums_all))
    length = (count_ref[z] - 1) * 64 + last_ref[z]
    valid = iota((1, LANES), 1) < length
    row = jnp.where(valid, logp[0], 0.0)
    ratio = jnp.sum(jnp.where(valid, logp[0] - logp[1], 0.0), axis=1, keepdims=True)
    out_ref[...] = rows_of(row, jnp.broadcast_to(ratio, (1, LANES)))

    for step in range(per_set):

        @pl.when(rollouts[step] != z)
        def _():
            await_bytes(local_stats.at[step], c0_send.at[step])

    @pl.when(a == z_set)
    def _():
        await_bytes(stats.at[pl.ds(0, chips - 1)], c1_send.at[0])
        await_bytes(stats, c1_send.at[1])


def body(
    nz,
    side,
    pages,
    page_table,
    page_count,
    last_len,
    targets,
    mix_key,
    w_key,
    w_value,
    ln_gain,
    ln_bias,
    head,
):
    chips = side * side
    per_set = nz // side
    width = chips * LANES
    units = w_key.shape[2]
    rows = head.shape[1]
    vmem = pl.BlockSpec(memory_space=pltpu.VMEM)
    hbm = pl.BlockSpec(memory_space=pl.ANY)
    dma = pltpu.SemaphoreType.DMA
    batches = len(BATCHES[nz])
    share = LANES // (2 * chips)
    semaphores = [6, 6, 14, (), ()]
    semaphores += [4] * 2 + [per_set] * 2 + [side] * 8
    semaphores += [(), (), (), batches, 2, (2, batches), (), (2, batches)]
    semaphores += [per_set] * 2 + [(), (2, side), (2, 2), (2, 2, 2), 2, (2, 2)]
    semaphores += [per_set, (), 2, (2, side)]
    result = pl.pallas_call(
        functools.partial(kernel, nz, side),
        out_shape=jax.ShapeDtypeStruct((8, LANES), F32),
        in_specs=[hbm] * 11,
        out_specs=vmem,
        scratch_shapes=[
            pltpu.SMEM(page_table.shape[::-1], jnp.int32),
            pltpu.SMEM(page_count.shape, jnp.int32),
            pltpu.SMEM(last_len.shape, jnp.int32),
            pltpu.VMEM(pages.shape, BF16),
            pltpu.VMEM(mix_key.shape, F32),
            pltpu.VMEM(ln_gain.shape, F32),
            pltpu.VMEM(ln_bias.shape, F32),
            pltpu.VMEM(pages.shape[1:], BF16),
            pltpu.VMEM(mix_key.shape, F32),
            pltpu.VMEM((nz, 1, LANES), jnp.int32),
            pltpu.VMEM((2, rows, head.shape[2]), BF16),
            pltpu.VMEM((width, 2 * side * LANES), BF16),
            pltpu.VMEM((width, 2 * units), BF16),
            pltpu.VMEM((2 * units, width), BF16),
            pltpu.VMEM((side * 4, 64, LANES), BF16),
            pltpu.VMEM((per_set, 2, 64, LANES), BF16),
            pltpu.VMEM((per_set, 2, 64, LANES), BF16),
            pltpu.VMEM((side, side, LANES, LANES), BF16),
            pltpu.VMEM((LANES, width), BF16),
            pltpu.VMEM((LANES, 2 * units), BF16),
            pltpu.VMEM((side, side, LANES, LANES), F32),
            pltpu.VMEM((side, side, LANES, LANES), F32),
            pltpu.VMEM((side, LANES, LANES), F32),
            pltpu.VMEM((side, LANES, LANES), F32),
            pltpu.VMEM((chips, 8, LANES), F32),
            pltpu.VMEM((per_set, LANES, LANES), BF16),
            pltpu.VMEM((per_set, LANES, width), BF16),
            pltpu.VMEM((side, per_set * LANES, 2 * LANES), F32),
            pltpu.VMEM((per_set, 8, LANES), F32),
            pltpu.VMEM((nz, 8, LANES), F32),
            pltpu.VMEM((2, side, 8, LANES), F32),
        ]
        + [dma(size if isinstance(size, tuple) else (size,)) for size in semaphores],
        compiler_params=pltpu.CompilerParams(
            collective_id=0, has_side_effects=True, vmem_limit_bytes=VMEM_LIMIT
        ),
    )(
        page_table.T,
        page_count,
        last_len,
        pages,
        mix_key,
        targets,
        ln_gain,
        ln_bias,
        w_key,
        w_value,
        head,
    )
    start = lax.axis_index("tensor") * share
    return lax.dynamic_slice(result, (0, start), (1, share)), result[1, 0:1]


def solution(mesh):
    nz = mesh.shape["dp"]
    side = {32: 4, 8: 2}[mesh.shape["tensor"]]
    specs = (
        P(None, "dp", None, "tensor"),
        P(),
        P(),
        P(),
        P("dp", None),
        P(None, "tensor"),
        P(None, None, "tensor"),
        P(None, "tensor", None),
        P(),
        P(),
        P(None, "dp", "tensor"),
    )
    return jax.shard_map(
        functools.partial(body, nz, side),
        mesh=mesh,
        in_specs=specs,
        out_specs=(P("dp", "tensor"), P("dp")),
        check_vma=False,
    )
```
